256 devices in a mesh: tok: 8 (over y, x_hi), hid: 32 (over x_lo, z, core).
Axes of the slice: x: 4 (x_hi: 2, x_lo: 2; x = x_hi * 2 + x_lo), y: 4, z: 8, core: 2. Of those that a mesh axis runs over, the one named last changes fastest.
Arguments:
- activations: bfloat16 [8192, 4096], P('tok', 'hid'), may hold values from -6 to 6
- gate_weight: bfloat16 [4096, 14336], P(None, 'hid'), may hold values from -0.09375 to 0.09375
- up_weight: bfloat16 [4096, 14336], P(None, 'hid'), may hold values from -0.09375 to 0.09375
- row_signs: int32 [8192], P('tok'), may hold values from 0 to 1
- row_scales: float32 [8192], P('tok'), may hold values from 0.25 to 4
- kept_rows: int32 [512], P('tok'), may hold values from 0 to 1023, as said below
Outputs:
- gram_matrix: float32 [512, 512], P('tok')
The draws below stay inside these ranges and needn't reach their ends.
Inputs may be any that keep to these rules, and one draw needn't show every extreme that they name: `kept_rows`: within each aligned block of 64 entries the values are distinct.
All inputs are finite; a program needn't handle non-finite values.
Results may differ from the reference program's by a relative error of at most 0.0014.
Values may be sent and summed in bfloat16 or wider, within the bound.
A program may use at most 64 MiB of HBM per device.

```python
import math
import jax
import jax.numpy as jnp
from jax import lax

D = 4096
FF = 14336
TOK_DEV = 1024
KEPT = 64
TOKENS = 8192
KEPT_TOTAL = 512


def draw_kept_rows(key, part):
    shard_keys = jax.random.split(key, KEPT_TOTAL // KEPT)
    chosen = jax.vmap(lambda single: jax.random.permutation(single, TOK_DEV)[:KEPT])(shard_keys)
    return chosen.reshape(KEPT_TOTAL).astype(jnp.int32)


def touch_ends(result, rng, least, high):
    dims = result.shape
    spot = [jax.random.randint(jax.random.fold_in(rng, axis), (), 0, dims[axis]) for axis in range(len(dims))]
    result = result.at[tuple(spot)].set(least)
    longest = dims.index(max(dims))
    spot[longest] = (spot[longest] + 1) % dims[longest]
    return result.at[tuple(spot)].set(high)


def level_of(key, extent, pieces, low, top_value):
    def one(axis_at, shards_of):
        draws = jax.random.uniform(jax.random.fold_in(jax.random.fold_in(key, 6), axis_at), (shards_of,), jnp.float32, low / len(pieces), top_value / len(pieces))
        return jnp.repeat(jnp.exp(draws), extent[axis_at] // shards_of).reshape((-1,) + (1,) * (len(extent) - axis_at - 1))

    loudness = one(*pieces[0])
    for cut in pieces[1:]:
        loudness = loudness * one(*cut)
    return loudness


def bell_draw(own_key, shape, deviation, most, shards=(), held_as=jnp.bfloat16):
    entries = jax.random.normal(own_key, shape, jnp.float32) * deviation
    if len(shards) > 0:
        entries = level_of(own_key, shape, shards, -0.22, 0.18) * entries
    return jnp.clip(entries, min=-most, max=most).astype(held_as)


def setup_inputs(seed: int = 0) -> dict:
    key_list = jax.random.split(jax.random.key(seed), 7)
    activations = bell_draw(key_list[0], (TOKENS, D), 1.0, 6.0, ((0, 8), (1, 32)))
    gate_weight = bell_draw(key_list[1], (D, FF), D ** -0.5, 0.09375, ((1, 32),))
    up_weight = bell_draw(key_list[2], (D, FF), D ** -0.5, 0.09375, ((1, 32),))
    row_signs = touch_ends(jax.random.randint(key_list[3], (TOKENS,), 0, 2), jax.random.fold_in(key_list[3], 1), 0, 1).astype(jnp.int32)
    row_scales = jnp.clip(jnp.exp(math.log(4.0) - 2.7725887 * jax.random.uniform(key_list[4], (TOKENS,), jnp.float32) ** level_of(key_list[4], (TOKENS,), ((0, 8),), -0.2, 0.2)), 0.25, 4.0)
    kept_rows = draw_kept_rows(jax.random.fold_in(key_list[6], 71), 0)
    return dict(activations=activations, gate_weight=gate_weight, up_weight=up_weight, row_signs=row_signs, row_scales=row_scales, kept_rows=kept_rows)


def bit_parity(values):
    parity = jnp.zeros_like(values)
    for shift_count in range(16):
        parity = parity ^ ((values >> shift_count) & 1)
    return parity


def hadamard_signs(first_rows, columns):
    parity = bit_parity(first_rows[:, None] & columns[None, :])
    return 1 - 2 * parity


def reference(activations, gate_weight, up_weight, row_signs, row_scales, kept_rows):
    gate_proj = jnp.dot(activations, gate_weight, preferred_element_type=jnp.float32)
    up_proj = jnp.dot(activations, up_weight, preferred_element_type=jnp.float32)
    row_factor = (2 * row_signs - 1).astype(jnp.float32) * row_scales
    signed_hidden = (row_factor[:, None] * jax.nn.silu(gate_proj) * up_proj).astype(jnp.bfloat16)
    shard_count = KEPT_TOTAL // KEPT
    blocks = signed_hidden.astype(jnp.float32).reshape(shard_count, TOK_DEV, FF)
    inner_table = hadamard_signs(jnp.arange(TOK_DEV, dtype=jnp.int32), jnp.arange(TOK_DEV, dtype=jnp.int32)).astype(jnp.float32)
    outer_table = hadamard_signs(jnp.arange(shard_count, dtype=jnp.int32), jnp.arange(shard_count, dtype=jnp.int32)).astype(jnp.float32)
    local_rows = jnp.einsum('kl,jlf->jkf', inner_table, blocks, precision=lax.Precision.HIGHEST)
    transformed = jnp.einsum('ij,jkf->ikf', outer_table, local_rows, precision=lax.Precision.HIGHEST)
    transformed = transformed.reshape(TOKENS, FF) * (float(TOKENS) ** -0.5)
    picked = (jnp.arange(KEPT_TOTAL, dtype=jnp.int32) // KEPT) * TOK_DEV + kept_rows.astype(jnp.int32)
    sketch = transformed[picked].astype(jnp.bfloat16)
    gram_matrix = jnp.dot(sketch, sketch.T, preferred_element_type=jnp.float32) * (float(FF) ** -0.5)
    return gram_matrix
```

```python
import functools

import jax
import jax.numpy as jnp
from jax import lax
from jax.experimental import pallas as pl
from jax.experimental.pallas import tpu as pltpu
from jax.sharding import PartitionSpec as P

FF = 14336
MESH = pl.DeviceIdType.MESH
F32 = jnp.float32
BF16 = jnp.bfloat16
ROWS_STEP = 256


def bit_parity(value):
    for shift in (8, 4, 2, 1):
        value = value ^ (value >> shift)
    return value & 1


def diagonal_column(row, count):
    ids = lax.broadcasted_iota(jnp.int32, (count, count), 0)
    lanes = lax.broadcasted_iota(jnp.int32, (count, count), 1)
    spread = jnp.where(ids == lanes, jnp.broadcast_to(row, (count, count)), 0.0)
    return jnp.sum(spread, axis=1, keepdims=True)


def fused(
    tok_n, hid_n, row_scale, gram_scale,
    act_in, wg_in, wu_in, sgn_in, scl_in, kept_in, out_ref,
    act, wg, wu, accg, accu, fcol, table, hidden, sgn, scl, kept,
    part, got, sk, gs, gr, gf,
    load_sem, zs, zr, xs, xr, ss, sr, bulk_s, bulk_r,
):
    zn = hid_n // 4
    far = zn // 2
    tokens, width = act_in.shape
    half = tokens // 2
    rows_step = min(ROWS_STEP, half)
    depth = 2 * width
    kept_n = kept.shape[-1]
    tok = lax.axis_index("tok")
    hid = lax.axis_index("hid")
    core = lax.rem(hid, 2)
    here = lax.div(hid, 2)
    z = lax.rem(here, zn)
    col = lax.div(here, zn)
    way = 1 - 2 * core

    def chip(own, d):
        c = col if own else 1 - col
        return c * zn + lax.rem(z - d * way + 2 * zn, zn)

    def at_hid(q):
        return {"hid": q * 2 + core}

    ahead = at_hid(chip(True, -1))
    behind = at_hid(chip(True, 1))
    across = at_hid(chip(False, 0))
    sibling = {"hid": here * 2 + 1 - core}

    loads = [
        pltpu.make_async_copy(act_in.at[pl.ds(h * half, half), :], act.at[here, core, h], load_sem.at[h])
        for h in range(2)
    ]
    loads += [
        pltpu.make_async_copy(src, dst, load_sem.at[2 + i])
        for i, (src, dst) in enumerate(((kept_in, kept.at[tok]), (sgn_in, sgn), (scl_in, scl), (wg_in, wg), (wu_in, wu)))
    ]
    for load in loads:
        load.start()

    barrier = pltpu.get_barrier_semaphore()

    def greet_hid(i, carry):
        pl.semaphore_signal(barrier, inc=1, device_id={"hid": lax.rem(hid + i, hid_n)}, device_id_type=MESH)
        return carry

    def greet_tok(i, carry):
        pl.semaphore_signal(barrier, inc=1, device_id={"tok": lax.rem(tok + i, tok_n)}, device_id_type=MESH)
        return carry

    lax.fori_loop(1, hid_n, greet_hid, 0)
    lax.fori_loop(1, tok_n, greet_tok, 0)
    pl.semaphore_wait(barrier, hid_n + tok_n - 2)

    sends = []

    def send(ref, send_sem, recv_sem, device):
        copy = pltpu.make_async_remote_copy(
            src_ref=ref, dst_ref=ref, send_sem=send_sem, recv_sem=recv_sem, device_id=device, device_id_type=MESH
        )
        copy.start()
        sends.append(copy)

    def arrive(ref, send_sem, recv_sem):
        pltpu.make_async_remote_copy(
            src_ref=ref, dst_ref=ref, send_sem=send_sem, recv_sem=recv_sem, device_id=sibling, device_id_type=MESH
        ).wait_recv()

    def piece(item, d, c=None):
        return act.at[chip(item < 2, d), core if c is None else c, 0 if item in (0, 3) else 1]

    def slot(d):
        return d if d >= 0 else far - d

    def go_z(item, d):
        if 0 <= d < far:
            send(piece(item, d), zs.at[0, d, item], zr.at[0, d, item], ahead)
        if -(far - 1) < d <= 0:
            send(piece(item, d), zs.at[1, -d, item], zr.at[1, -d, item], behind)

    def from_z(item, d):
        if d > 0:
            arrive(piece(item, d), zs.at[0, d - 1, item], zr.at[0, d - 1, item])
        else:
            arrive(piece(item, d), zs.at[1, -d - 1, item], zr.at[1, -d - 1, item])

    def go_x(item, d):
        k = slot(d) if item == 0 else 2 * far
        send(piece(item, d), xs.at[k], xr.at[k], across)

    def from_x(item, d):
        k = slot(d) if item == 3 else 2 * far
        arrive(piece(item, d), xs.at[k], xr.at[k])

    def go_sibling(item, d):
        send(piece(item, d), ss.at[item, slot(d)], sr.at[item, slot(d)], sibling)

    def from_sibling(item, d):
        e = -d if abs(d) < far else d
        arrive(piece(item, d, 1 - core), ss.at[item, slot(e)], sr.at[item, slot(e)])

    def matmul(blocks, which, first=False):
        def tile(m, carry):
            rows = pl.ds(pl.multiple_of(m * rows_step, rows_step), rows_step)
            out_rows = pl.ds(pl.multiple_of(which * half + m * rows_step, rows_step), rows_step)
            left = jnp.concatenate([act[q, c, which, rows, :] for q in blocks for c in range(2)], axis=1)
            for weight, acc in ((wg, accg), (wu, accu)):
                right = jnp.concatenate(
                    [weight[pl.ds(pl.multiple_of(q * depth, depth), depth), :] for q in blocks], axis=0
                )
                product = jnp.dot(left, right, preferred_element_type=F32)
                acc[out_rows, :] = product if first else acc[out_rows, :] + product
            return carry

        lax.fori_loop(0, half // rows_step, tile, 0)

    def offsets(k):
        return [k] if k in (0, far) else [k, -k]

    def unit(items, which, first=False):
        for item, d in items:
            from_sibling(item, d)
        matmul([chip(item < 2, d) for item, d in items], which, first)

    for load in loads[:2]:
        load.wait()
    go_z(0, 0)
    go_x(1, 0)
    go_x(0, 0)
    go_z(1, 0)
    go_sibling(0, 0)
    go_sibling(1, 0)
    loads[2].wait()

    def send_kept(i, carry):
        pltpu.make_async_remote_copy(
            src_ref=kept.at[tok], dst_ref=kept.at[tok], send_sem=bulk_s.at[0], recv_sem=bulk_r.at[0],
            device_id={"tok": lax.rem(tok + i, tok_n)}, device_id_type=MESH,
        ).start()
        return carry

    lax.fori_loop(1, tok_n, send_kept, 0)

    def settle(ref, sem):
        pltpu.make_async_copy(ref, ref, sem).wait()

    from_x(2, 0)
    go_z(2, 0)
    go_sibling(2, 0)

    loads[3].wait()
    loads[4].wait()
    groups, lanes = sgn.shape
    factor = (2 * sgn[...] - 1).astype(F32) * scl[...]
    for g in range(groups):
        column = diagonal_column(factor[g : g + 1, :], lanes)
        fcol[g * lanes : (g + 1) * lanes, :] = jnp.broadcast_to(column, (lanes, fcol.shape[1]))

    loads[5].wait()
    loads[6].wait()

    def sign_rows(j, carry):
        owner = bit_parity(j & tok)
        column = diagonal_column(kept[j].astype(F32), kept_n).astype(jnp.int32)
        places = lax.broadcasted_iota(jnp.int32, (kept_n, tokens), 1)
        parity = bit_parity(jnp.broadcast_to(column, (kept_n, tokens)) & places) ^ owner
        table[pl.ds(pl.multiple_of(j * kept_n, kept_n), kept_n), :] = (1 - 2 * parity).astype(F32).astype(BF16)
        return carry

    for k in range(1, far + 1):
        near = offsets(k)
        before = offsets(k - 1)
        for d in near:
            from_z(0, d)
            go_z(0, d)
            go_x(0, d)
            go_sibling(0, d)
        if k == 1:
            unit([(0, 0)], 0, True)
        else:
            unit([(0, d) for d in before] + [(3, d) for d in offsets(k - 2)], 0)
        for d in near:
            from_z(1, d)
            go_z(1, d)
            go_sibling(1, d)
        for d in before:
            from_x(3, d)
            go_sibling(3, d)
        if k == 1:
            settle(kept.at[pl.ds(0, tok_n - 1)], bulk_s.at[0])
            settle(kept.at[pl.ds(0, tok_n - 1)], bulk_r.at[0])
            lax.fori_loop(0, tok_n, sign_rows, 0)
        for d in near:
            from_z(2, d)
            go_z(2, d)
            go_sibling(2, d)
        unit([(1, d) for d in before] + [(2, d) for d in before], 1, k == 1)
    from_x(3, far)
    go_sibling(3, far)
    unit([(0, far)] + [(3, d) for d in offsets(far - 1)], 0)
    unit([(1, far), (2, far)], 1)
    unit([(3, far)], 0)

    def activate(m, carry):
        rows = pl.ds(pl.multiple_of(m * 128, 128), 128)
        gate = accg[rows, :]
        silu = gate / (1.0 + jnp.exp(-gate))
        hidden[rows, :] = (fcol[rows, 0:1] * silu * accu[rows, :]).astype(BF16)
        return carry

    lax.fori_loop(0, tokens // 128, activate, 0)

    owners_step = max(tok_n // 2, 1)
    for b in range(tok_n // owners_step):
        rows = slice(b * owners_step * kept_n, (b + 1) * owners_step * kept_n)
        product = jnp.dot(table[rows, :], hidden[...], preferred_element_type=F32).astype(BF16)
        for i in range(owners_step):
            part[b * owners_step + i] = product[i * kept_n : (i + 1) * kept_n, :]

    def send_part(i, carry):
        peer = lax.rem(tok + i, tok_n)
        pltpu.make_async_remote_copy(
            src_ref=part.at[peer], dst_ref=got.at[tok], send_sem=bulk_s.at[1], recv_sem=bulk_r.at[1],
            device_id={"tok": peer}, device_id_type=MESH,
        ).start()
        return carry

    lax.fori_loop(1, tok_n, send_part, 0)
    got[tok] = part[tok]
    settle(got.at[pl.ds(0, tok_n - 1)], bulk_r.at[1])
    total = got[0].astype(F32)
    for j in range(1, tok_n):
        total = total + got[j].astype(F32)
    mine = (total * row_scale).astype(BF16)
    sk[tok] = mine

    def send_sketch(i, carry):
        pltpu.make_async_remote_copy(
            src_ref=sk.at[tok], dst_ref=sk.at[tok], send_sem=bulk_s.at[2], recv_sem=bulk_r.at[2],
            device_id={"tok": lax.rem(tok + i, tok_n)}, device_id_type=MESH,
        ).start()
        return carry

    lax.fori_loop(1, tok_n, send_sketch, 0)
    settle(sk.at[pl.ds(0, tok_n - 1)], bulk_r.at[2])
    every = sk[...].reshape(tok_n * kept_n, sk.shape[-1])
    gram = lax.dot_general(mine, every, (((1,), (1,)), ((), ())), preferred_element_type=F32) * gram_scale

    tile_rows, tile_lanes = gs.shape[1:]
    across_n = gram.shape[1] // tile_lanes
    for t in range(hid_n):
        a, b = divmod(t, across_n)
        gs[t] = gram[a * tile_rows : (a + 1) * tile_rows, b * tile_lanes : (b + 1) * tile_lanes]

    def send_tile(i, carry):
        peer = lax.rem(hid + i, hid_n)
        pltpu.make_async_remote_copy(
            src_ref=gs.at[peer], dst_ref=gr.at[hid], send_sem=bulk_s.at[3], recv_sem=bulk_r.at[3],
            device_id={"hid": peer}, device_id_type=MESH,
        ).start()
        return carry

    lax.fori_loop(1, hid_n, send_tile, 0)
    gr[hid] = gs[hid]
    settle(gr.at[pl.ds(0, hid_n - 1)], bulk_r.at[3])
    gf[hid] = jnp.sum(gr[...], axis=0)

    def send_sum(i, carry):
        pltpu.make_async_remote_copy(
            src_ref=gf.at[hid], dst_ref=gf.at[hid], send_sem=bulk_s.at[4], recv_sem=bulk_r.at[4],
            device_id={"hid": lax.rem(hid + i, hid_n)}, device_id_type=MESH,
        ).start()
        return carry

    lax.fori_loop(1, hid_n, send_sum, 0)
    for copy in sends:
        copy.wait_send()
    settle(part.at[pl.ds(0, tok_n - 1)], bulk_s.at[1])
    settle(sk.at[pl.ds(0, tok_n - 1)], bulk_s.at[2])
    settle(gs.at[pl.ds(0, hid_n - 1)], bulk_s.at[3])
    settle(gf.at[pl.ds(0, hid_n - 1)], bulk_r.at[4])
    for t in range(hid_n):
        a, b = divmod(t, across_n)
        out_ref[a * tile_rows : (a + 1) * tile_rows, b * tile_lanes : (b + 1) * tile_lanes] = gf[t]
    settle(gf.at[pl.ds(0, hid_n - 1)], bulk_s.at[4])


def per_device(tok_n, hid_n, activations, gate_weight, up_weight, row_signs, row_scales, kept_rows):
    tokens, width = activations.shape
    depth, units = gate_weight.shape
    kept_n = kept_rows.shape[0]
    zn = hid_n // 4
    far = zn // 2
    lanes = min(128, tokens)
    tile_lanes = kept_n * kept_n * tok_n // 8 // hid_n
    hbm = pl.BlockSpec(memory_space=pl.ANY)
    dma = pltpu.SemaphoreType.DMA
    return pl.pallas_call(
        functools.partial(fused, tok_n, hid_n, float(tokens * tok_n) ** -0.5, float(FF) ** -0.5),
        out_shape=jax.ShapeDtypeStruct((kept_n, kept_n * tok_n), F32),
        in_specs=[hbm] * 6,
        out_specs=pl.BlockSpec(memory_space=pltpu.VMEM),
        scratch_shapes=[
            pltpu.VMEM((hid_n // 2, 2, 2, tokens // 2, width), BF16),
            pltpu.VMEM((depth, units), BF16),
            pltpu.VMEM((depth, units), BF16),
            pltpu.VMEM((tokens, units), F32),
            pltpu.VMEM((tokens, units), F32),
            pltpu.VMEM((tokens, 128), F32),
            pltpu.VMEM((kept_n * tok_n, tokens), BF16),
            pltpu.VMEM((tokens, units), BF16),
            pltpu.VMEM((tokens // lanes, lanes), jnp.int32),
            pltpu.VMEM((tokens // lanes, lanes), F32),
            pltpu.VMEM((tok_n, 1, kept_n), jnp.int32),
            pltpu.VMEM((tok_n, kept_n, units), BF16),
            pltpu.VMEM((tok_n, kept_n, units), BF16),
            pltpu.VMEM((tok_n, kept_n, units), BF16),
            pltpu.VMEM((hid_n, 8, tile_lanes), F32),
            pltpu.VMEM((hid_n, 8, tile_lanes), F32),
            pltpu.VMEM((hid_n, 8, tile_lanes), F32),
            dma((7,)),
            dma((2, far, 3)),
            dma((2, far, 3)),
            dma((2 * far + 1,)),
            dma((2 * far + 1,)),
            dma((4, 2 * far)),
            dma((4, 2 * far)),
            dma((5,)),
            dma((5,)),
        ],
        compiler_params=pltpu.CompilerParams(
            collective_id=0, has_side_effects=True, vmem_limit_bytes=60 * 1024 * 1024
        ),
        name="sketch_gram",
    )(
        activations, gate_weight, up_weight,
        row_signs.reshape(-1, lanes), row_scales.reshape(-1, lanes), kept_rows.reshape(1, -1),
    )


def solution(mesh):
    placed = (P("tok", "hid"), P(None, "hid"), P(None, "hid"), P("tok"), P("tok"), P("tok"))
    return jax.shard_map(
        functools.partial(per_device, mesh.shape["tok"], mesh.shape["hid"]),
        mesh=mesh, in_specs=placed, out_specs=P("tok", None), check_vma=False,
    )
```

```python
import functools

import jax
import jax.numpy as jnp
from jax import lax
from jax.experimental import pallas as pl
from jax.experimental.pallas import tpu as pltpu
from jax.sharding import PartitionSpec as P

FF = 14336
MESH = pl.DeviceIdType.MESH
F32 = jnp.float32
BF16 = jnp.bfloat16
ROWS_STEP = 256


def bit_parity(value):
    for shift in (8, 4, 2, 1):
        value = value ^ (value >> shift)
    return value & 1


def diagonal_column(row, count):
    ids = lax.broadcasted_iota(jnp.int32, (count, count), 0)
    lanes = lax.broadcasted_iota(jnp.int32, (count, count), 1)
    spread = jnp.where(ids == lanes, jnp.broadcast_to(row, (count, count)), 0.0)
    return jnp.sum(spread, axis=1, keepdims=True)


def fused(
    tok_n, hid_n, row_scale, gram_scale,
    act_in, wg_in, wu_in, sgn_in, scl_in, kept_in, out_ref,
    act, weights, acc, table, hidden, sgn, scl, kept,
    part, got, sk, gs, gr, gf,
    load_sem, zs, zr, xs, xr, ss, sr, bulk_s, bulk_r,
):
    zn = hid_n // 4
    far = zn // 2
    tokens, width = act_in.shape
    half = tokens // 2
    rows_step = min(ROWS_STEP, half)
    depth = 2 * width
    kept_n = kept.shape[-1]
    units = wg_in.shape[0]
    tok = lax.axis_index("tok")
    hid = lax.axis_index("hid")
    core = lax.rem(hid, 2)
    here = lax.div(hid, 2)
    z = lax.rem(here, zn)
    col = lax.div(here, zn)
    way = 1 - 2 * core

    def chip(own, d):
        c = col if own else 1 - col
        return c * zn + lax.rem(z - d * way + 2 * zn, zn)

    def at_hid(q):
        return {"hid": q * 2 + core}

    ahead = at_hid(chip(True, -1))
    behind = at_hid(chip(True, 1))
    across = at_hid(chip(False, 0))
    sibling = {"hid": here * 2 + 1 - core}

    loads = [
        pltpu.make_async_copy(act_in.at[pl.ds(h * half, half), :], act.at[here, core, h], load_sem.at[h])
        for h in range(2)
    ]
    loads += [
        pltpu.make_async_copy(src, dst, load_sem.at[2 + i])
        for i, (src, dst) in enumerate(((kept_in, kept.at[tok]), (sgn_in, sgn), (scl_in, scl),
                                         (wg_in, weights.at[pl.ds(0, units), :]), (wu_in, weights.at[pl.ds(units, units), :])))
    ]
    for load in loads:
        load.start()

    barrier = pltpu.get_barrier_semaphore()

    def greet_hid(i, carry):
        pl.semaphore_signal(barrier, inc=1, device_id={"hid": lax.rem(hid + i, hid_n)}, device_id_type=MESH)
        return carry

    def greet_tok(i, carry):
        pl.semaphore_signal(barrier, inc=1, device_id={"tok": lax.rem(tok + i, tok_n)}, device_id_type=MESH)
        return carry

    lax.fori_loop(1, hid_n, greet_hid, 0)
    lax.fori_loop(1, tok_n, greet_tok, 0)
    pl.semaphore_wait(barrier, hid_n + tok_n - 2)

    sends = []

    def send(ref, send_sem, recv_sem, device):
        copy = pltpu.make_async_remote_copy(
            src_ref=ref, dst_ref=ref, send_sem=send_sem, recv_sem=recv_sem, device_id=device, device_id_type=MESH
        )
        copy.start()
        sends.append(copy)

    def arrive(ref, send_sem, recv_sem):
        pltpu.make_async_remote_copy(
            src_ref=ref, dst_ref=ref, send_sem=send_sem, recv_sem=recv_sem, device_id=sibling, device_id_type=MESH
        ).wait_recv()

    def piece(item, d, c=None):
        return act.at[chip(item < 2, d), core if c is None else c, 0 if item in (0, 3) else 1]

    def slot(d):
        return d if d >= 0 else far - d

    def go_z(item, d):
        if 0 <= d < far:
            send(piece(item, d), zs.at[0, d, item], zr.at[0, d, item], ahead)
        if -(far - 1) < d <= 0:
            send(piece(item, d), zs.at[1, -d, item], zr.at[1, -d, item], behind)

    def from_z(item, d):
        if d > 0:
            arrive(piece(item, d), zs.at[0, d - 1, item], zr.at[0, d - 1, item])
        else:
            arrive(piece(item, d), zs.at[1, -d - 1, item], zr.at[1, -d - 1, item])

    def go_x(item, d):
        k = slot(d) if item == 0 else 2 * far
        send(piece(item, d), xs.at[k], xr.at[k], across)

    def from_x(item, d):
        k = slot(d) if item == 3 else 2 * far
        arrive(piece(item, d), xs.at[k], xr.at[k])

    def go_sibling(item, d):
        send(piece(item, d), ss.at[item, slot(d)], sr.at[item, slot(d)], sibling)

    def from_sibling(item, d):
        e = -d if abs(d) < far else d
        arrive(piece(item, d, 1 - core), ss.at[item, slot(e)], sr.at[item, slot(e)])

    def matmul(blocks, which, first=False):
        def tile(m, carry):
            rows = pl.ds(pl.multiple_of(m * rows_step, rows_step), rows_step)
            columns = pl.ds(pl.multiple_of(which * half + m * rows_step, rows_step), rows_step)
            left = jnp.concatenate(
                [weights[:, pl.ds(pl.multiple_of(q * depth, depth), depth)] for q in blocks], axis=1
            )
            right = jnp.concatenate([act[q, c, which, rows, :] for q in blocks for c in range(2)], axis=1)
            product = lax.dot_general(left, right, (((1,), (1,)), ((), ())), preferred_element_type=F32)
            acc[:, columns] = product if first else acc[:, columns] + product
            return carry

        lax.fori_loop(0, half // rows_step, tile, 0)

    def offsets(k):
        return [k] if k in (0, far) else [k, -k]

    def unit(items, which, first=False):
        for item, d in items:
            from_sibling(item, d)
        matmul([chip(item < 2, d) for item, d in items], which, first)

    for load in loads[:2]:
        load.wait()
    go_z(0, 0)
    go_x(1, 0)
    go_x(0, 0)
    go_z(1, 0)
    go_sibling(0, 0)
    go_sibling(1, 0)
    loads[2].wait()

    def send_kept(i, carry):
        pltpu.make_async_remote_copy(
            src_ref=kept.at[tok], dst_ref=kept.at[tok], send_sem=bulk_s.at[0], recv_sem=bulk_r.at[0],
            device_id={"tok": lax.rem(tok + i, tok_n)}, device_id_type=MESH,
        ).start()
        return carry

    lax.fori_loop(1, tok_n, send_kept, 0)

    def settle(ref, sem):
        pltpu.make_async_copy(ref, ref, sem).wait()

    from_x(2, 0)
    go_z(2, 0)
    go_sibling(2, 0)

    loads[3].wait()
    loads[4].wait()
    loads[5].wait()
    loads[6].wait()

    def sign_rows(j, carry):
        owner = bit_parity(j & tok)
        column = diagonal_column(kept[j].astype(F32), kept_n).astype(jnp.int32)
        places = lax.broadcasted_iota(jnp.int32, (kept_n, tokens), 1)
        parity = bit_parity(jnp.broadcast_to(column, (kept_n, tokens)) & places) ^ owner
        table[pl.ds(pl.multiple_of(j * kept_n, kept_n), kept_n), :] = (1 - 2 * parity).astype(F32).astype(BF16)
        return carry

    for k in range(1, far + 1):
        near = offsets(k)
        before = offsets(k - 1)
        for d in near:
            from_z(0, d)
            go_z(0, d)
            go_x(0, d)
            go_sibling(0, d)
        if k == 1:
            unit([(0, 0)], 0, True)
        else:
            unit([(0, d) for d in before] + [(3, d) for d in offsets(k - 2)], 0)
        for d in near:
            from_z(1, d)
            go_z(1, d)
            go_sibling(1, d)
        for d in before:
            from_x(3, d)
            go_sibling(3, d)
        if k == 1:
            settle(kept.at[pl.ds(0, tok_n - 1)], bulk_s.at[0])
            settle(kept.at[pl.ds(0, tok_n - 1)], bulk_r.at[0])
            lax.fori_loop(0, tok_n, sign_rows, 0)
        for d in near:
            from_z(2, d)
            go_z(2, d)
            go_sibling(2, d)
        unit([(1, d) for d in before] + [(2, d) for d in before], 1, k == 1)
    from_x(3, far)
    go_sibling(3, far)
    unit([(0, far)] + [(3, d) for d in offsets(far - 1)], 0)
    unit([(1, far), (2, far)], 1)
    unit([(3, far)], 0)

    def activate(m, carry):
        gate = acc[pl.ds(pl.multiple_of(m * 64, 64), 64), :]
        up = acc[pl.ds(pl.multiple_of(units + m * 64, 64), 64), :]
        factor = (2 * sgn[...] - 1).astype(F32) * scl[...]
        silu = gate / (1.0 + jnp.exp(-gate))
        hidden[pl.ds(pl.multiple_of(m * 64, 64), 64), :] = (factor * silu * up).astype(BF16)
        return carry

    lax.fori_loop(0, units // 64, activate, 0)

    owners_step = max(tok_n // 2, 1)
    for b in range(tok_n // owners_step):
        rows = slice(b * owners_step * kept_n, (b + 1) * owners_step * kept_n)
        product = lax.dot_general(
            table[rows, :], hidden[...], (((1,), (1,)), ((), ())), preferred_element_type=F32
        ).astype(BF16)
        for i in range(owners_step):
            part[b * owners_step + i] = product[i * kept_n : (i + 1) * kept_n, :]

    def send_part(i, carry):
        peer = lax.rem(tok + i, tok_n)
        pltpu.make_async_remote_copy(
            src_ref=part.at[peer], dst_ref=got.at[tok], send_sem=bulk_s.at[1], recv_sem=bulk_r.at[1],
            device_id={"tok": peer}, device_id_type=MESH,
        ).start()
        return carry

    lax.fori_loop(1, tok_n, send_part, 0)
    got[tok] = part[tok]
    settle(got.at[pl.ds(0, tok_n - 1)], bulk_r.at[1])
    total = got[0].astype(F32)
    for j in range(1, tok_n):
        total = total + got[j].astype(F32)
    mine = (total * row_scale).astype(BF16)
    sk[tok] = mine

    def send_sketch(i, carry):
        pltpu.make_async_remote_copy(
            src_ref=sk.at[tok], dst_ref=sk.at[tok], send_sem=bulk_s.at[2], recv_sem=bulk_r.at[2],
            device_id={"tok": lax.rem(tok + i, tok_n)}, device_id_type=MESH,
        ).start()
        return carry

    lax.fori_loop(1, tok_n, send_sketch, 0)
    settle(sk.at[pl.ds(0, tok_n - 1)], bulk_r.at[2])
    every = sk[...].reshape(tok_n * kept_n, sk.shape[-1])
    gram = lax.dot_general(mine, every, (((1,), (1,)), ((), ())), preferred_element_type=F32) * gram_scale

    tile_rows, tile_lanes = gs.shape[1:]
    across_n = gram.shape[1] // tile_lanes
    for t in range(hid_n):
        a, b = divmod(t, across_n)
        gs[t] = gram[a * tile_rows : (a + 1) * tile_rows, b * tile_lanes : (b + 1) * tile_lanes]

    def send_tile(i, carry):
        peer = lax.rem(hid + i, hid_n)
        pltpu.make_async_remote_copy(
            src_ref=gs.at[peer], dst_ref=gr.at[hid], send_sem=bulk_s.at[3], recv_sem=bulk_r.at[3],
            device_id={"hid": peer}, device_id_type=MESH,
        ).start()
        return carry

    lax.fori_loop(1, hid_n, send_tile, 0)
    gr[hid] = gs[hid]
    settle(gr.at[pl.ds(0, hid_n - 1)], bulk_r.at[3])
    gf[hid] = jnp.sum(gr[...], axis=0)

    def send_sum(i, carry):
        pltpu.make_async_remote_copy(
            src_ref=gf.at[hid], dst_ref=gf.at[hid], send_sem=bulk_s.at[4], recv_sem=bulk_r.at[4],
            device_id={"hid": lax.rem(hid + i, hid_n)}, device_id_type=MESH,
        ).start()
        return carry

    lax.fori_loop(1, hid_n, send_sum, 0)
    for copy in sends:
        copy.wait_send()
    settle(part.at[pl.ds(0, tok_n - 1)], bulk_s.at[1])
    settle(sk.at[pl.ds(0, tok_n - 1)], bulk_s.at[2])
    settle(gs.at[pl.ds(0, hid_n - 1)], bulk_s.at[3])
    settle(gf.at[pl.ds(0, hid_n - 1)], bulk_r.at[4])
    for t in range(hid_n):
        a, b = divmod(t, across_n)
        out_ref[a * tile_rows : (a + 1) * tile_rows, b * tile_lanes : (b + 1) * tile_lanes] = gf[t]
    settle(gf.at[pl.ds(0, hid_n - 1)], bulk_s.at[4])


def per_device(tok_n, hid_n, activations, gate_weight, up_weight, row_signs, row_scales, kept_rows):
    tokens, width = activations.shape
    depth, units = gate_weight.shape
    kept_n = kept_rows.shape[0]
    zn = hid_n // 4
    far = zn // 2
    tile_lanes = kept_n * kept_n * tok_n // 8 // hid_n
    hbm = pl.BlockSpec(memory_space=pl.ANY)
    dma = pltpu.SemaphoreType.DMA
    return pl.pallas_call(
        functools.partial(fused, tok_n, hid_n, float(tokens * tok_n) ** -0.5, float(FF) ** -0.5),
        out_shape=jax.ShapeDtypeStruct((kept_n, kept_n * tok_n), F32),
        in_specs=[hbm] * 6,
        out_specs=pl.BlockSpec(memory_space=pltpu.VMEM),
        scratch_shapes=[
            pltpu.VMEM((hid_n // 2, 2, 2, tokens // 2, width), BF16),
            pltpu.VMEM((2 * units, depth), BF16),
            pltpu.VMEM((2 * units, tokens), F32),
            pltpu.VMEM((kept_n * tok_n, tokens), BF16),
            pltpu.VMEM((units, tokens), BF16),
            pltpu.VMEM((1, tokens), jnp.int32),
            pltpu.VMEM((1, tokens), F32),
            pltpu.VMEM((tok_n, 1, kept_n), jnp.int32),
            pltpu.VMEM((tok_n, kept_n, units), BF16),
            pltpu.VMEM((tok_n, kept_n, units), BF16),
            pltpu.VMEM((tok_n, kept_n, units), BF16),
            pltpu.VMEM((hid_n, 8, tile_lanes), F32),
            pltpu.VMEM((hid_n, 8, tile_lanes), F32),
            pltpu.VMEM((hid_n, 8, tile_lanes), F32),
            dma((7,)),
            dma((2, far, 3)),
            dma((2, far, 3)),
            dma((2 * far + 1,)),
            dma((2 * far + 1,)),
            dma((4, 2 * far)),
            dma((4, 2 * far)),
            dma((5,)),
            dma((5,)),
        ],
        compiler_params=pltpu.CompilerParams(
            collective_id=0, has_side_effects=True, vmem_limit_bytes=60 * 1024 * 1024
        ),
        name="sketch_gram",
    )(
        activations, gate_weight.T, up_weight.T,
        row_signs.reshape(1, -1), row_scales.reshape(1, -1), kept_rows.reshape(1, -1),
    )


def solution(mesh):
    placed = (P("tok", "hid"), P(None, "hid"), P(None, "hid"), P("tok"), P("tok"), P("tok"))
    return jax.shard_map(
        functools.partial(per_device, mesh.shape["tok"], mesh.shape["hid"]),
        mesh=mesh, in_specs=placed, out_specs=P("tok", None), check_vma=False,
    )
```

```python
import functools

import jax
import jax.numpy as jnp
from jax import lax
from jax.experimental import pallas as pl
from jax.experimental.pallas import tpu as pltpu
from jax.sharding import PartitionSpec as P

FF = 14336
MESH = pl.DeviceIdType.MESH
F32 = jnp.float32
BF16 = jnp.bfloat16
ROWS_STEP = 256


def bit_parity(value):
    for shift in (8, 4, 2, 1):
        value = value ^ (value >> shift)
    return value & 1


def diagonal_column(row, count):
    ids = lax.broadcasted_iota(jnp.int32, (count, count), 0)
    lanes = lax.broadcasted_iota(jnp.int32, (count, count), 1)
    spread = jnp.where(ids == lanes, jnp.broadcast_to(row, (count, count)), 0.0)
    return jnp.sum(spread, axis=1, keepdims=True)


def fused(
    tok_n, hid_n, row_scale, gram_scale,
    act_in, wg_in, wu_in, sgn_in, scl_in, kept_in, out_ref,
    act, weights, acc, table, hidden, sgn, scl, kept,
    part, got, sk, gs, gr, gf,
    load_sem, zs, zr, xs, xr, ss, sr, bulk_s, bulk_r,
):
    zn = hid_n // 4
    far = zn // 2
    tokens, width = act_in.shape
    half = tokens // 2
    rows_step = min(ROWS_STEP, half)
    depth = 2 * width
    kept_n = kept.shape[-1]
    units = wg_in.shape[0]
    tok = lax.axis_index("tok")
    hid = lax.axis_index("hid")
    core = lax.rem(hid, 2)
    here = lax.div(hid, 2)
    z = lax.rem(here, zn)
    col = lax.div(here, zn)
    way = 1 - 2 * core

    def chip(own, d):
        c = col if own else 1 - col
        return c * zn + lax.rem(z - d * way + 2 * zn, zn)

    def at_hid(q):
        return {"hid": q * 2 + core}

    ahead = at_hid(chip(True, -1))
    behind = at_hid(chip(True, 1))
    across = at_hid(chip(False, 0))
    sibling = {"hid": here * 2 + 1 - core}

    loads = [
        pltpu.make_async_copy(act_in.at[pl.ds(h * half, half), :], act.at[here, core, h], load_sem.at[h])
        for h in range(2)
    ]
    loads += [
        pltpu.make_async_copy(src, dst, load_sem.at[2 + i])
        for i, (src, dst) in enumerate(((kept_in, kept.at[tok]), (sgn_in, sgn), (scl_in, scl),
                                         (wg_in, weights.at[pl.ds(0, units), :]), (wu_in, weights.at[pl.ds(units, units), :])))
    ]
    for load in loads:
        load.start()

    barrier = pltpu.get_barrier_semaphore()

    def greet(i, carry):
        pl.semaphore_signal(barrier, inc=1, device_id={"tok": lax.rem(tok + i, tok_n)}, device_id_type=MESH)
        return carry

    for neighbour in (ahead, behind, across, sibling):
        pl.semaphore_signal(barrier, inc=1, device_id=neighbour, device_id_type=MESH)
    lax.fori_loop(1, tok_n, greet, 0)
    pl.semaphore_wait(barrier, 4 + tok_n - 1)

    sends = []

    def send(ref, send_sem, recv_sem, device):
        copy = pltpu.make_async_remote_copy(
            src_ref=ref, dst_ref=ref, send_sem=send_sem, recv_sem=recv_sem, device_id=device, device_id_type=MESH
        )
        copy.start()
        sends.append(copy)

    def arrive(ref, send_sem, recv_sem):
        pltpu.make_async_remote_copy(
            src_ref=ref, dst_ref=ref, send_sem=send_sem, recv_sem=recv_sem, device_id=sibling, device_id_type=MESH
        ).wait_recv()

    def piece(item, d, c=None):
        return act.at[chip(item < 2, d), core if c is None else c, 0 if item in (0, 3) else 1]

    def slot(d):
        return d if d >= 0 else far - d

    def go_z(item, d):
        if 0 <= d < far:
            send(piece(item, d), zs.at[0, d, item], zr.at[0, d, item], ahead)
        if -(far - 1) < d <= 0:
            send(piece(item, d), zs.at[1, -d, item], zr.at[1, -d, item], behind)

    def from_z(item, d):
        if d > 0:
            arrive(piece(item, d), zs.at[0, d - 1, item], zr.at[0, d - 1, item])
        else:
            arrive(piece(item, d), zs.at[1, -d - 1, item], zr.at[1, -d - 1, item])

    def go_x(item, d):
        k = slot(d) if item == 0 else 2 * far
        send(piece(item, d), xs.at[k], xr.at[k], across)

    def from_x(item, d):
        k = slot(d) if item == 3 else 2 * far
        arrive(piece(item, d), xs.at[k], xr.at[k])

    def go_sibling(item, d):
        send(piece(item, d), ss.at[item, slot(d)], sr.at[item, slot(d)], sibling)

    def from_sibling(item, d):
        e = -d if abs(d) < far else d
        arrive(piece(item, d, 1 - core), ss.at[item, slot(e)], sr.at[item, slot(e)])

    def matmul(blocks, which, first=False):
        def tile(m, carry):
            rows = pl.ds(pl.multiple_of(m * rows_step, rows_step), rows_step)
            columns = pl.ds(pl.multiple_of(which * half + m * rows_step, rows_step), rows_step)
            left = jnp.concatenate(
                [weights[:, pl.ds(pl.multiple_of(q * depth, depth), depth)] for q in blocks], axis=1
            )
            right = jnp.concatenate([act[q, c, which, rows, :] for q in blocks for c in range(2)], axis=1)
            product = lax.dot_general(left, right, (((1,), (1,)), ((), ())), preferred_element_type=F32)
            acc[:, columns] = product if first else acc[:, columns] + product
            return carry

        lax.fori_loop(0, half // rows_step, tile, 0)

    def offsets(k):
        return [k] if k in (0, far) else [k, -k]

    def unit(items, which, first=False):
        for item, d in items:
            from_sibling(item, d)
        matmul([chip(item < 2, d) for item, d in items], which, first)

    for load in loads[:2]:
        load.wait()
    go_z(0, 0)
    go_x(1, 0)
    go_z(1, 0)
    go_x(0, 0)
    go_sibling(0, 0)
    go_sibling(1, 0)
    loads[2].wait()

    def send_kept(i, carry):
        pltpu.make_async_remote_copy(
            src_ref=kept.at[tok], dst_ref=kept.at[tok], send_sem=bulk_s.at[0], recv_sem=bulk_r.at[0],
            device_id={"tok": lax.rem(tok + i, tok_n)}, device_id_type=MESH,
        ).start()
        return carry

    lax.fori_loop(1, tok_n, send_kept, 0)

    def settle(ref, sem):
        pltpu.make_async_copy(ref, ref, sem).wait()

    def sign_rows(j, carry):
        owner = bit_parity(j & tok)
        column = diagonal_column(kept[j].astype(F32), kept_n).astype(jnp.int32)
        places = lax.broadcasted_iota(jnp.int32, (kept_n, tokens), 1)
        parity = bit_parity(jnp.broadcast_to(column, (kept_n, tokens)) & places) ^ owner
        table[pl.ds(pl.multiple_of(j * kept_n, kept_n), kept_n), :] = (1 - 2 * parity).astype(F32).astype(BF16)
        return carry

    def ring(r):
        return [(1 + (r + 1) % 2, d) for d in offsets((r + 1) // 2)]

    for k in range(1, 2 * far + 1):
        if k <= far:
            for d in offsets(k):
                from_z(0, d)
                go_z(0, d)
                go_x(0, d)
                go_sibling(0, d)
            if k == 1:
                from_x(2, 0)
                go_sibling(2, 0)
                go_z(2, 0)
            else:
                for item, d in ring(k - 1):
                    go_z(item, d)
        for item, d in ring(k):
            from_z(item, d)
            if k >= far:
                go_z(item, d)
            go_sibling(item, d)
        if k <= far + 1:
            for d in offsets(k - 1):
                from_x(3, d)
                go_sibling(3, d)
        if k == 1:
            settle(kept.at[pl.ds(0, tok_n - 1)], bulk_s.at[0])
            settle(kept.at[pl.ds(0, tok_n - 1)], bulk_r.at[0])
            lax.fori_loop(0, tok_n, sign_rows, 0)
            for load in loads[3:]:
                load.wait()
            unit([(0, 0), (0, 1), (0, -1)], 0, True)
        elif k <= far + 2:
            unit(([(0, d) for d in offsets(k)] if k <= far else []) + [(3, d) for d in offsets(k - 2)], 0)
        if k == 2:
            unit([(1, 0), (2, 0)] + ring(1), 1, True)
        elif k % 2 == 0:
            unit(ring(k - 2) + (ring(k - 1) if k < 2 * far else []), 1)
    unit(ring(2 * far - 1) + ring(2 * far), 1)

    def activate(m, carry):
        gate = acc[pl.ds(pl.multiple_of(m * 64, 64), 64), :]
        up = acc[pl.ds(pl.multiple_of(units + m * 64, 64), 64), :]
        factor = (2 * sgn[...] - 1).astype(F32) * scl[...]
        silu = gate / (1.0 + jnp.exp(-gate))
        hidden[pl.ds(pl.multiple_of(m * 64, 64), 64), :] = (factor * silu * up).astype(BF16)
        return carry

    lax.fori_loop(0, units // 64, activate, 0)

    strips = units // 128

    def packed(rows):
        tail = rows[:, strips * 128 :]
        tail = jnp.concatenate([tail[: kept_n // 2], tail[kept_n // 2 :]], axis=1)
        return jnp.concatenate([rows[:, c * 128 : (c + 1) * 128] for c in range(strips)] + [tail], axis=0)

    def unpacked(strip):
        blocks = [strip[c * kept_n : (c + 1) * kept_n, :] for c in range(strips)]
        tail = strip[strips * kept_n :, :]
        return jnp.concatenate(blocks + [jnp.concatenate([tail[:, :64], tail[:, 64:]], axis=0)], axis=1)

    owners_step = max(tok_n // 2, 1)
    for b in range(tok_n // owners_step):
        rows = slice(b * owners_step * kept_n, (b + 1) * owners_step * kept_n)
        product = lax.dot_general(
            table[rows, :], hidden[...], (((1,), (1,)), ((), ())), preferred_element_type=F32
        )
        for i in range(owners_step):
            part[b * owners_step + i] = packed(product[i * kept_n : (i + 1) * kept_n, :]).astype(BF16)

    def send_part(i, carry):
        peer = lax.rem(tok + i, tok_n)
        pltpu.make_async_remote_copy(
            src_ref=part.at[peer], dst_ref=got.at[tok], send_sem=bulk_s.at[1], recv_sem=bulk_r.at[1],
            device_id={"tok": peer}, device_id_type=MESH,
        ).start()
        return carry

    lax.fori_loop(1, tok_n, send_part, 0)
    got[tok] = part[tok]
    settle(got.at[pl.ds(0, tok_n - 1)], bulk_r.at[1])
    total = got[0].astype(F32)
    for j in range(1, tok_n):
        total = total + got[j].astype(F32)
    mine = (total * row_scale).astype(BF16)
    sk[tok] = mine

    def send_sketch(i, carry):
        pltpu.make_async_remote_copy(
            src_ref=sk.at[tok], dst_ref=sk.at[tok], send_sem=bulk_s.at[2], recv_sem=bulk_r.at[2],
            device_id={"tok": lax.rem(tok + i, tok_n)}, device_id_type=MESH,
        ).start()
        return carry

    lax.fori_loop(1, tok_n, send_sketch, 0)
    settle(sk.at[pl.ds(0, tok_n - 1)], bulk_r.at[2])
    every = jnp.concatenate([unpacked(sk[j].astype(F32)).astype(BF16) for j in range(tok_n)], axis=0)
    gram = lax.dot_general(unpacked(mine.astype(F32)).astype(BF16), every, (((1,), (1,)), ((), ())), preferred_element_type=F32) * gram_scale

    tile_rows, tile_lanes = gs.shape[1:]
    across_n = gram.shape[1] // tile_lanes
    for t in range(hid_n):
        a, b = divmod(t, across_n)
        gs[t] = gram[a * tile_rows : (a + 1) * tile_rows, b * tile_lanes : (b + 1) * tile_lanes]

    def send_tile(i, carry):
        peer = lax.rem(hid + i, hid_n)
        pltpu.make_async_remote_copy(
            src_ref=gs.at[peer], dst_ref=gr.at[hid], send_sem=bulk_s.at[3], recv_sem=bulk_r.at[3],
            device_id={"hid": peer}, device_id_type=MESH,
        ).start()
        return carry

    lax.fori_loop(1, hid_n, send_tile, 0)
    gr[hid] = gs[hid]
    settle(gr.at[pl.ds(0, hid_n - 1)], bulk_r.at[3])
    gf[hid] = jnp.sum(gr[...], axis=0)

    def send_sum(i, carry):
        pltpu.make_async_remote_copy(
            src_ref=gf.at[hid], dst_ref=gf.at[hid], send_sem=bulk_s.at[4], recv_sem=bulk_r.at[4],
            device_id={"hid": lax.rem(hid + i, hid_n)}, device_id_type=MESH,
        ).start()
        return carry

    lax.fori_loop(1, hid_n, send_sum, 0)
    for copy in sends:
        copy.wait_send()
    settle(part.at[pl.ds(0, tok_n - 1)], bulk_s.at[1])
    settle(sk.at[pl.ds(0, tok_n - 1)], bulk_s.at[2])
    settle(gs.at[pl.ds(0, hid_n - 1)], bulk_s.at[3])
    settle(gf.at[pl.ds(0, hid_n - 1)], bulk_r.at[4])
    for t in range(hid_n):
        a, b = divmod(t, across_n)
        out_ref[a * tile_rows : (a + 1) * tile_rows, b * tile_lanes : (b + 1) * tile_lanes] = gf[t]
    settle(gf.at[pl.ds(0, hid_n - 1)], bulk_s.at[4])


def per_device(tok_n, hid_n, activations, gate_weight, up_weight, row_signs, row_scales, kept_rows):
    tokens, width = activations.shape
    depth, units = gate_weight.shape
    kept_n = kept_rows.shape[0]
    zn = hid_n // 4
    far = zn // 2
    tile_lanes = kept_n * kept_n * tok_n // 8 // hid_n
    hbm = pl.BlockSpec(memory_space=pl.ANY)
    dma = pltpu.SemaphoreType.DMA
    return pl.pallas_call(
        functools.partial(fused, tok_n, hid_n, float(tokens * tok_n) ** -0.5, float(FF) ** -0.5),
        out_shape=jax.ShapeDtypeStruct((kept_n, kept_n * tok_n), F32),
        in_specs=[hbm] * 6,
        out_specs=pl.BlockSpec(memory_space=pltpu.VMEM),
        scratch_shapes=[
            pltpu.VMEM((hid_n // 2, 2, 2, tokens // 2, width), BF16),
            pltpu.VMEM((2 * units, depth), BF16),
            pltpu.VMEM((2 * units, tokens), F32),
            pltpu.VMEM((kept_n * tok_n, tokens), BF16),
            pltpu.VMEM((units, tokens), BF16),
            pltpu.VMEM((1, tokens), jnp.int32),
            pltpu.VMEM((1, tokens), F32),
            pltpu.VMEM((tok_n, 1, kept_n), jnp.int32),
            pltpu.VMEM((tok_n, kept_n * units // 128, 128), BF16),
            pltpu.VMEM((tok_n, kept_n * units // 128, 128), BF16),
            pltpu.VMEM((tok_n, kept_n * units // 128, 128), BF16),
            pltpu.VMEM((hid_n, 8, tile_lanes), F32),
            pltpu.VMEM((hid_n, 8, tile_lanes), F32),
            pltpu.VMEM((hid_n, 8, tile_lanes), F32),
            dma((7,)),
            dma((2, far, 3)),
            dma((2, far, 3)),
            dma((2 * far + 1,)),
            dma((2 * far + 1,)),
            dma((4, 2 * far)),
            dma((4, 2 * far)),
            dma((5,)),
            dma((5,)),
        ],
        compiler_params=pltpu.CompilerParams(
            collective_id=0, has_side_effects=True, vmem_limit_bytes=60 * 1024 * 1024
        ),
        name="sketch_gram",
    )(
        activations, gate_weight.T, up_weight.T,
        row_signs.reshape(1, -1), row_scales.reshape(1, -1), kept_rows.reshape(1, -1),
    )


def solution(mesh):
    placed = (P("tok", "hid"), P(None, "hid"), P(None, "hid"), P("tok"), P("tok"), P("tok"))
    return jax.shard_map(
        functools.partial(per_device, mesh.shape["tok"], mesh.shape["hid"]),
        mesh=mesh, in_specs=placed, out_specs=P("tok", None), check_vma=False,
    )
```

```python
import functools

import jax
import jax.numpy as jnp
from jax import lax
from jax.experimental import pallas as pl
from jax.experimental.pallas import tpu as pltpu
from jax.sharding import PartitionSpec as P

FF = 14336
MESH = pl.DeviceIdType.MESH
F32 = jnp.float32
BF16 = jnp.bfloat16
ROWS_STEP = 256


def bit_parity(value):
    for shift in (8, 4, 2, 1):
        value = value ^ (value >> shift)
    return value & 1


def diagonal_column(row, count):
    ids = lax.broadcasted_iota(jnp.int32, (count, count), 0)
    lanes = lax.broadcasted_iota(jnp.int32, (count, count), 1)
    spread = jnp.where(ids == lanes, jnp.broadcast_to(row, (count, count)), 0.0)
    return jnp.sum(spread, axis=1, keepdims=True)


def fused(
    tok_n, hid_n, row_scale, gram_scale,
    act_in, wg_in, wu_in, sgn_in, scl_in, kept_in, out_ref,
    act, weights, acc, table, hidden, sgn, scl, kept,
    part, got, sk, gs, gr, gf,
    load_sem, zs, zr, xs, xr, ss, sr, bulk_s, bulk_r,
):
    zn = hid_n // 4
    far = zn // 2
    tokens, width = act_in.shape
    half = tokens // 2
    rows_step = min(ROWS_STEP, half)
    depth = 2 * width
    kept_n = kept.shape[-1]
    units = wg_in.shape[0]
    tok = lax.axis_index("tok")
    hid = lax.axis_index("hid")
    core = lax.rem(hid, 2)
    here = lax.div(hid, 2)
    z = lax.rem(here, zn)
    col = lax.div(here, zn)
    way = 1 - 2 * core

    def chip(own, d):
        c = col if own else 1 - col
        return c * zn + lax.rem(z - d * way + 2 * zn, zn)

    def at_hid(q):
        return {"hid": q * 2 + core}

    ahead = at_hid(chip(True, -1))
    behind = at_hid(chip(True, 1))
    across = at_hid(chip(False, 0))
    sibling = {"hid": here * 2 + 1 - core}

    def ring_order(n):
        return sorted(range(n), key=lambda step: -min(step, n - step))

    hid_peers = [
        (lax.rem(col + a, 2) * zn + lax.rem(z + step, zn)) * 2 + lax.rem(core + c, 2)
        for step in ring_order(zn) for a in (1, 0) for c in (1, 0) if step or a or c
    ]
    yn = tok_n // 2
    tok_peers = [
        lax.rem(lax.div(tok, 2) + step, yn) * 2 + lax.rem(tok + a, 2)
        for a in (1, 0) for step in ring_order(yn) if step or a
    ]

    loads = [
        pltpu.make_async_copy(act_in.at[pl.ds(h * half, half), :], act.at[here, core, h], load_sem.at[h])
        for h in range(2)
    ]
    loads += [
        pltpu.make_async_copy(src, dst, load_sem.at[2 + i])
        for i, (src, dst) in enumerate(((kept_in, kept.at[tok]), (sgn_in, sgn), (scl_in, scl),
                                         (wg_in, weights.at[pl.ds(0, units), :]), (wu_in, weights.at[pl.ds(units, units), :])))
    ]
    for load in loads:
        load.start()

    barrier = pltpu.get_barrier_semaphore()

    for peer in tok_peers:
        pl.semaphore_signal(barrier, inc=1, device_id={"tok": peer}, device_id_type=MESH)

    for neighbour in (ahead, behind, across, sibling):
        pl.semaphore_signal(barrier, inc=1, device_id=neighbour, device_id_type=MESH)
    pl.semaphore_wait(barrier, 4 + tok_n - 1)

    sends = []

    def send(ref, send_sem, recv_sem, device):
        copy = pltpu.make_async_remote_copy(
            src_ref=ref, dst_ref=ref, send_sem=send_sem, recv_sem=recv_sem, device_id=device, device_id_type=MESH
        )
        copy.start()
        sends.append(copy)

    def arrive(ref, send_sem, recv_sem):
        pltpu.make_async_remote_copy(
            src_ref=ref, dst_ref=ref, send_sem=send_sem, recv_sem=recv_sem, device_id=sibling, device_id_type=MESH
        ).wait_recv()

    def piece(item, d, c=None):
        return act.at[chip(item < 2, d), core if c is None else c, 0 if item in (0, 3) else 1]

    def slot(d):
        return d if d >= 0 else far - d

    def go_z(item, d):
        if 0 <= d < far:
            send(piece(item, d), zs.at[0, d, item], zr.at[0, d, item], ahead)
        if -(far - 1) < d <= 0:
            send(piece(item, d), zs.at[1, -d, item], zr.at[1, -d, item], behind)

    def from_z(item, d):
        if d > 0:
            arrive(piece(item, d), zs.at[0, d - 1, item], zr.at[0, d - 1, item])
        else:
            arrive(piece(item, d), zs.at[1, -d - 1, item], zr.at[1, -d - 1, item])

    def go_x(item, d):
        k = slot(d) if item == 0 else 2 * far
        send(piece(item, d), xs.at[k], xr.at[k], across)

    def from_x(item, d):
        k = slot(d) if item == 3 else 2 * far
        arrive(piece(item, d), xs.at[k], xr.at[k])

    def go_sibling(item, d):
        send(piece(item, d), ss.at[item, slot(d)], sr.at[item, slot(d)], sibling)

    def from_sibling(item, d):
        e = -d if abs(d) < far else d
        arrive(piece(item, d, 1 - core), ss.at[item, slot(e)], sr.at[item, slot(e)])

    def matmul(blocks, which, first=False):
        def tile(m, carry):
            rows = pl.ds(pl.multiple_of(m * rows_step, rows_step), rows_step)
            columns = pl.ds(pl.multiple_of(which * half + m * rows_step, rows_step), rows_step)
            left = jnp.concatenate(
                [weights[:, pl.ds(pl.multiple_of(q * depth, depth), depth)] for q in blocks], axis=1
            )
            right = jnp.concatenate([act[q, c, which, rows, :] for q in blocks for c in range(2)], axis=1)
            product = lax.dot_general(left, right, (((1,), (1,)), ((), ())), preferred_element_type=F32)
            acc[:, columns] = product if first else acc[:, columns] + product
            return carry

        lax.fori_loop(0, half // rows_step, tile, 0)

    def offsets(k):
        return [k] if k in (0, far) else [k, -k]

    def unit(items, which, first=False):
        for item, d in items:
            from_sibling(item, d)
        matmul([chip(item < 2, d) for item, d in items], which, first)

    for load in loads[:2]:
        load.wait()
    go_z(0, 0)
    go_x(1, 0)
    go_z(1, 0)
    go_x(0, 0)
    go_sibling(0, 0)
    go_sibling(1, 0)
    loads[2].wait()

    for peer in tok_peers:
        pltpu.make_async_remote_copy(
            src_ref=kept.at[tok], dst_ref=kept.at[tok], send_sem=bulk_s.at[0], recv_sem=bulk_r.at[0],
            device_id={"tok": peer}, device_id_type=MESH,
        ).start()

    def settle(ref, sem):
        pltpu.make_async_copy(ref, ref, sem).wait()

    def sign_rows(j, carry):
        owner = bit_parity(j & tok)
        column = diagonal_column(kept[j].astype(F32), kept_n).astype(jnp.int32)
        places = lax.broadcasted_iota(jnp.int32, (kept_n, tokens), 1)
        parity = bit_parity(jnp.broadcast_to(column, (kept_n, tokens)) & places) ^ owner
        table[pl.ds(pl.multiple_of(j * kept_n, kept_n), kept_n), :] = (1 - 2 * parity).astype(F32).astype(BF16)
        return carry

    def ring(r):
        return [(1 + (r + 1) % 2, d) for d in offsets((r + 1) // 2)]

    for k in range(1, 2 * far + 1):
        if k <= far:
            for d in offsets(k):
                from_z(0, d)
                go_z(0, d)
                go_x(0, d)
                go_sibling(0, d)
            if k == 1:
                from_x(2, 0)
                go_sibling(2, 0)
                go_z(2, 0)
            else:
                for item, d in ring(k - 1):
                    go_z(item, d)
        for item, d in ring(k):
            from_z(item, d)
            if k >= far:
                go_z(item, d)
            go_sibling(item, d)
        if k <= far + 1:
            for d in offsets(k - 1):
                from_x(3, d)
                go_sibling(3, d)
        if k == 1:
            settle(kept.at[pl.ds(0, tok_n - 1)], bulk_s.at[0])
            settle(kept.at[pl.ds(0, tok_n - 1)], bulk_r.at[0])
            lax.fori_loop(0, tok_n, sign_rows, 0)
            for load in loads[3:]:
                load.wait()
            unit([(0, 0), (0, 1), (0, -1)], 0, True)
        elif k <= far + 2:
            unit(([(0, d) for d in offsets(k)] if k <= far else []) + [(3, d) for d in offsets(k - 2)], 0)
        if k == 2:
            unit([(1, 0), (2, 0)] + ring(1), 1, True)
        elif k % 2 == 0:
            unit(ring(k - 2) + (ring(k - 1) if k < 2 * far else []), 1)
    unit(ring(2 * far - 1) + ring(2 * far), 1)

    def activate(m, carry):
        gate = acc[pl.ds(pl.multiple_of(m * 64, 64), 64), :]
        up = acc[pl.ds(pl.multiple_of(units + m * 64, 64), 64), :]
        factor = (2 * sgn[...] - 1).astype(F32) * scl[...]
        silu = gate / (1.0 + jnp.exp(-gate))
        hidden[pl.ds(pl.multiple_of(m * 64, 64), 64), :] = (factor * silu * up).astype(BF16)
        return carry

    lax.fori_loop(0, units // 64, activate, 0)

    strips = units // 128

    def packed(rows):
        tail = rows[:, strips * 128 :]
        tail = jnp.concatenate([tail[: kept_n // 2], tail[kept_n // 2 :]], axis=1)
        return jnp.concatenate([rows[:, c * 128 : (c + 1) * 128] for c in range(strips)] + [tail], axis=0)

    def unpacked(strip):
        blocks = [strip[c * kept_n : (c + 1) * kept_n, :] for c in range(strips)]
        tail = strip[strips * kept_n :, :]
        return jnp.concatenate(blocks + [jnp.concatenate([tail[:, :64], tail[:, 64:]], axis=0)], axis=1)

    owners_step = max(tok_n // 2, 1)
    for b in range(tok_n // owners_step):
        rows = slice(b * owners_step * kept_n, (b + 1) * owners_step * kept_n)
        product = lax.dot_general(
            table[rows, :], hidden[...], (((1,), (1,)), ((), ())), preferred_element_type=F32
        )
        for i in range(owners_step):
            part[b * owners_step + i] = packed(product[i * kept_n : (i + 1) * kept_n, :]).astype(BF16)

    for peer in tok_peers:
        pltpu.make_async_remote_copy(
            src_ref=part.at[peer], dst_ref=got.at[tok], send_sem=bulk_s.at[1], recv_sem=bulk_r.at[1],
            device_id={"tok": peer}, device_id_type=MESH,
        ).start()
    got[tok] = part[tok]
    settle(got.at[pl.ds(0, tok_n - 1)], bulk_r.at[1])
    total = got[0].astype(F32)
    for j in range(1, tok_n):
        total = total + got[j].astype(F32)
    mine = (total * row_scale).astype(BF16)
    sk[tok] = mine

    for peer in tok_peers:
        pltpu.make_async_remote_copy(
            src_ref=sk.at[tok], dst_ref=sk.at[tok], send_sem=bulk_s.at[2], recv_sem=bulk_r.at[2],
            device_id={"tok": peer}, device_id_type=MESH,
        ).start()
    settle(sk.at[pl.ds(0, tok_n - 1)], bulk_r.at[2])
    every = jnp.concatenate([unpacked(sk[j].astype(F32)).astype(BF16) for j in range(tok_n)], axis=0)
    gram = lax.dot_general(unpacked(mine.astype(F32)).astype(BF16), every, (((1,), (1,)), ((), ())), preferred_element_type=F32) * gram_scale

    tile_rows, tile_lanes = gs.shape[1:]
    across_n = gram.shape[1] // tile_lanes
    for t in range(hid_n):
        a, b = divmod(t, across_n)
        gs[t] = gram[a * tile_rows : (a + 1) * tile_rows, b * tile_lanes : (b + 1) * tile_lanes]

    for peer in hid_peers:
        pltpu.make_async_remote_copy(
            src_ref=gs.at[peer], dst_ref=gr.at[hid], send_sem=bulk_s.at[3], recv_sem=bulk_r.at[3],
            device_id={"hid": peer}, device_id_type=MESH,
        ).start()
    gr[hid] = gs[hid]
    settle(gr.at[pl.ds(0, hid_n - 1)], bulk_r.at[3])
    gf[hid] = jnp.sum(gr[...], axis=0)

    for peer in hid_peers:
        pltpu.make_async_remote_copy(
            src_ref=gf.at[hid], dst_ref=gf.at[hid], send_sem=bulk_s.at[4], recv_sem=bulk_r.at[4],
            device_id={"hid": peer}, device_id_type=MESH,
        ).start()
    for copy in sends:
        copy.wait_send()
    settle(part.at[pl.ds(0, tok_n - 1)], bulk_s.at[1])
    settle(sk.at[pl.ds(0, tok_n - 1)], bulk_s.at[2])
    settle(gs.at[pl.ds(0, hid_n - 1)], bulk_s.at[3])
    settle(gf.at[pl.ds(0, hid_n - 1)], bulk_r.at[4])
    for t in range(hid_n):
        a, b = divmod(t, across_n)
        out_ref[a * tile_rows : (a + 1) * tile_rows, b * tile_lanes : (b + 1) * tile_lanes] = gf[t]
    settle(gf.at[pl.ds(0, hid_n - 1)], bulk_s.at[4])


def per_device(tok_n, hid_n, activations, gate_weight, up_weight, row_signs, row_scales, kept_rows):
    tokens, width = activations.shape
    depth, units = gate_weight.shape
    kept_n = kept_rows.shape[0]
    zn = hid_n // 4
    far = zn // 2
    tile_lanes = kept_n * kept_n * tok_n // 8 // hid_n
    hbm = pl.BlockSpec(memory_space=pl.ANY)
    dma = pltpu.SemaphoreType.DMA
    return pl.pallas_call(
        functools.partial(fused, tok_n, hid_n, float(tokens * tok_n) ** -0.5, float(FF) ** -0.5),
        out_shape=jax.ShapeDtypeStruct((kept_n, kept_n * tok_n), F32),
        in_specs=[hbm] * 6,
        out_specs=pl.BlockSpec(memory_space=pltpu.VMEM),
        scratch_shapes=[
            pltpu.VMEM((hid_n // 2, 2, 2, tokens // 2, width), BF16),
            pltpu.VMEM((2 * units, depth), BF16),
            pltpu.VMEM((2 * units, tokens), F32),
            pltpu.VMEM((kept_n * tok_n, tokens), BF16),
            pltpu.VMEM((units, tokens), BF16),
            pltpu.VMEM((1, tokens), jnp.int32),
            pltpu.VMEM((1, tokens), F32),
            pltpu.VMEM((tok_n, 1, kept_n), jnp.int32),
            pltpu.VMEM((tok_n, kept_n * units // 128, 128), BF16),
            pltpu.VMEM((tok_n, kept_n * units // 128, 128), BF16),
            pltpu.VMEM((tok_n, kept_n * units // 128, 128), BF16),
            pltpu.VMEM((hid_n, 8, tile_lanes), F32),
            pltpu.VMEM((hid_n, 8, tile_lanes), F32),
            pltpu.VMEM((hid_n, 8, tile_lanes), F32),
            dma((7,)),
            dma((2, far, 3)),
            dma((2, far, 3)),
            dma((2 * far + 1,)),
            dma((2 * far + 1,)),
            dma((4, 2 * far)),
            dma((4, 2 * far)),
            dma((5,)),
            dma((5,)),
        ],
        compiler_params=pltpu.CompilerParams(
            collective_id=0, has_side_effects=True, vmem_limit_bytes=60 * 1024 * 1024
        ),
        name="sketch_gram",
    )(
        activations, gate_weight.T, up_weight.T,
        row_signs.reshape(1, -1), row_scales.reshape(1, -1), kept_rows.reshape(1, -1),
    )


def solution(mesh):
    placed = (P("tok", "hid"), P(None, "hid"), P(None, "hid"), P("tok"), P("tok"), P("tok"))
    return jax.shard_map(
        functools.partial(per_device, mesh.shape["tok"], mesh.shape["hid"]),
        mesh=mesh, in_specs=placed, out_specs=P("tok", None), check_vma=False,
    )
```

```python
import functools

import jax
import jax.numpy as jnp
from jax import lax
from jax.experimental import pallas as pl
from jax.experimental.pallas import tpu as pltpu
from jax.sharding import PartitionSpec as P

FF = 14336
MESH = pl.DeviceIdType.MESH
F32 = jnp.float32
BF16 = jnp.bfloat16


def bit_parity(value):
    for shift in (8, 4, 2, 1):
        value = value ^ (value >> shift)
    return value & 1


def diagonal_column(row, count):
    ids = lax.broadcasted_iota(jnp.int32, (count, count), 0)
    lanes = lax.broadcasted_iota(jnp.int32, (count, count), 1)
    spread = jnp.where(ids == lanes, jnp.broadcast_to(row, (count, count)), 0.0)
    return jnp.sum(spread, axis=1, keepdims=True)


def fused(
    tok_n, hid_n, row_scale, gram_scale,
    act_in, wg_in, wu_in, sgn_in, scl_in, kept_in, out_ref,
    act, guest, weights, acc, table, hidden, sgn, scl, factor, kept,
    part, got, sk, gs, gr, gf,
    load_sem, zs, zr, xs, xr, cs, cr, ss, sr, bulk_s, bulk_r,
):
    zn = hid_n // 4
    far = zn // 2
    tokens, width = act_in.shape
    block = tokens // 4
    depth = 2 * width
    kept_n = kept.shape[-1]
    units = wg_in.shape[0]
    tok = lax.axis_index("tok")
    hid = lax.axis_index("hid")
    core = lax.rem(hid, 2)
    here = lax.div(hid, 2)
    z = lax.rem(here, zn)
    col = lax.div(here, zn)
    way = 1 - 2 * core

    def chip(own, d):
        c = col if own else 1 - col
        return c * zn + lax.rem(z - d * way + 2 * zn, zn)

    def at_hid(q):
        return {"hid": q * 2 + core}

    ahead = at_hid(chip(True, -1))
    behind = at_hid(chip(True, 1))
    across = at_hid(chip(False, 0))
    sibling = {"hid": here * 2 + 1 - core}
    other_tok = tok + 1 - 2 * lax.rem(tok, 2)
    cross = {"tok": other_tok, "hid": chip(False, 0) * 2 + core}
    keep = 2 * col
    give = 2 - 2 * col

    def ring_order(n):
        return sorted(range(n), key=lambda step: -min(step, n - step))

    hid_peers = [
        (lax.rem(col + a, 2) * zn + lax.rem(z + step, zn)) * 2 + lax.rem(core + c, 2)
        for step in ring_order(zn) for a in (1, 0) for c in (1, 0) if step or a or c
    ]
    yn = tok_n // 2
    tok_peers = [
        lax.rem(lax.div(tok, 2) + step, yn) * 2 + lax.rem(tok + a, 2)
        for a in (1, 0) for step in ring_order(yn) if step or a
    ]

    loads = [
        pltpu.make_async_copy(act_in.at[pl.ds(b * block, block), :], act.at[here, core, b], load_sem.at[b])
        for b in range(4)
    ]
    loads += [
        pltpu.make_async_copy(src, dst, load_sem.at[4 + i])
        for i, (src, dst) in enumerate(((kept_in, kept.at[tok]), (sgn_in, sgn), (scl_in, scl),
                                         (wg_in, weights.at[pl.ds(0, units), :]), (wu_in, weights.at[pl.ds(units, units), :])))
    ]
    for load in loads:
        load.start()

    barrier = pltpu.get_barrier_semaphore()

    for peer in tok_peers:
        pl.semaphore_signal(barrier, inc=1, device_id={"tok": peer}, device_id_type=MESH)

    for neighbour in (ahead, behind, across, sibling, cross):
        pl.semaphore_signal(barrier, inc=1, device_id=neighbour, device_id_type=MESH)
    pl.semaphore_wait(barrier, 5 + tok_n - 1)

    sends = []

    def send(ref, send_sem, recv_sem, device, there=None):
        copy = pltpu.make_async_remote_copy(
            src_ref=ref, dst_ref=ref if there is None else there, send_sem=send_sem, recv_sem=recv_sem,
            device_id=device, device_id_type=MESH,
        )
        copy.start()
        sends.append(copy)

    def arrive(ref, send_sem, recv_sem):
        pltpu.make_async_remote_copy(
            src_ref=ref, dst_ref=ref, send_sem=send_sem, recv_sem=recv_sem, device_id=sibling, device_id_type=MESH
        ).wait_recv()

    def slot(d):
        return d if d >= 0 else far - d

    def z_piece(item, d):
        shard = act.at[chip(item < 2, d), core]
        return shard.at[pl.ds(0, 3)] if item == 0 else shard.at[3]

    def go_z(item, d):
        if 0 <= d < far:
            send(z_piece(item, d), zs.at[0, d, item], zr.at[0, d, item], ahead)
        if -(far - 1) < d <= 0:
            send(z_piece(item, d), zs.at[1, -d, item], zr.at[1, -d, item], behind)

    def from_z(item, d):
        way_in = (0, d - 1) if d > 0 else (1, -d - 1)
        arrive(z_piece(item, d), zs.at[*way_in, item], zr.at[*way_in, item])

    def go_x(kind, d):
        b = (give, 1, 3)[kind]
        send(act.at[chip(True, d), core, b], xs.at[kind, slot(d)], xr.at[kind, slot(d)], across)

    def from_x(kind, d):
        b = (keep, 1, 3)[kind]
        arrive(act.at[chip(False, d), core, b], xs.at[kind, slot(d)], xr.at[kind, slot(d)])

    def go_cross(kind, d):
        q = chip(kind == 0, d)
        send(act.at[q, core, keep], cs.at[kind, slot(d)], cr.at[kind, slot(d)], cross, guest.at[q, core])

    def from_cross(kind, d):
        arrive(guest.at[chip(kind == 1, d), core], cs.at[kind, slot(d)], cr.at[kind, slot(d)])

    def shared(item, d, c):
        if item >= 5:
            return guest.at[chip(item == 6, d), c]
        shard = act.at[chip(item < 2, d), c]
        if item == 0:
            return shard.at[pl.ds(col, 2)]
        return shard.at[(None, 3, 3, keep, 1)[item]]

    def go_sibling(item, d):
        send(shared(item, d, core), ss.at[item, slot(d)], sr.at[item, slot(d)], sibling)

    def from_sibling(item, d):
        e = -d if abs(d) < far else d
        arrive(shared(item, d, 1 - core), ss.at[item, slot(e)], sr.at[item, slot(e)])

    def offsets(k):
        return [k] if k in (0, far) else [k, -k]

    def multiply(shards, read, start, first):
        left = jnp.concatenate(
            [weights[:, pl.ds(pl.multiple_of(q * depth, depth), depth)] for q in shards], axis=1
        )
        right = jnp.concatenate([read(q, c) for q in shards for c in range(2)], axis=1)
        product = lax.dot_general(left, right, (((1,), (1,)), ((), ())), preferred_element_type=F32)
        columns = pl.ds(start, block)
        acc[:, columns] = product if first else acc[:, columns] + product

    started = set()

    def unit(group, items):
        for item, d in items:
            for part_item in (3, 4) if item == 3 else (item,):
                from_sibling(part_item, d)
        shards = [chip(item in (0, 1, 6), d) for item, d in items]
        first = group not in started
        started.add(group)
        if group == "main":
            def tile(m, carry):
                multiply(shards, lambda q, c: act[q, c, col + m], pl.multiple_of(m * block, block), first)
                return carry

            lax.fori_loop(0, 2, tile, 0)
        elif group == "near":
            multiply(shards, lambda q, c: act[q, c, 3], 2 * block, first)
        else:
            multiply(shards, lambda q, c: guest[q, c], 3 * block, first)

    def settle(ref, sem):
        pltpu.make_async_copy(ref, ref, sem).wait()

    for load in loads[:4]:
        load.wait()
    go_z(0, 0)
    go_x(2, 0)
    go_cross(0, 0)
    go_x(0, 0)
    go_z(1, 0)
    go_x(1, 0)
    go_sibling(0, 0)
    go_sibling(1, 0)
    for load in loads[4:7]:
        load.wait()
    for peer in tok_peers:
        pltpu.make_async_remote_copy(
            src_ref=kept.at[tok], dst_ref=kept.at[tok], send_sem=bulk_s.at[0], recv_sem=bulk_r.at[0],
            device_id={"tok": peer}, device_id_type=MESH,
        ).start()
    factor[0] = (2 * sgn[...] - 1).astype(F32) * scl[...]
    factor_copy = pltpu.make_async_remote_copy(
        src_ref=factor.at[0], dst_ref=factor.at[1], send_sem=bulk_s.at[5], recv_sem=bulk_r.at[5],
        device_id=cross, device_id_type=MESH,
    )
    factor_copy.start()

    spots = lax.broadcasted_iota(jnp.int32, (kept_n, tokens), 1)
    places = spots + jnp.where(spots < 2 * block, col * block, jnp.where(spots < 3 * block, block, (give - 3) * block))

    def sign_rows(j, carry):
        owner = jnp.where(spots < 3 * block, bit_parity(j & tok), bit_parity(j & other_tok))
        column = diagonal_column(kept[j].astype(F32), kept_n).astype(jnp.int32)
        parity = bit_parity(jnp.broadcast_to(column, (kept_n, tokens)) & places) ^ owner
        table[pl.ds(pl.multiple_of(j * kept_n, kept_n), kept_n), :] = (1 - 2 * parity).astype(F32).astype(BF16)
        return carry

    def ring(r):
        return [(1 + (r + 1) % 2, d) for d in offsets((r + 1) // 2)]

    waiting = {"main": [(0, 0)], "near": [(1, 0)], "guest": []}

    def work(ready, least):
        for group in ("main", "near", "guest"):
            items = ready[group]
            if len(items) >= least:
                unit(group, items)
                waiting[group] = waiting[group][len(items) :]

    def partner_blocks(k):
        for d in offsets(k - 1):
            from_x(0, d)
            go_cross(1, d)
            go_sibling(3, d)

    def own_blocks(k):
        for d in offsets(k):
            from_z(0, d)
            go_z(0, d)
            go_x(0, d)
            go_cross(0, d)
            if k < far - 1:
                go_x(1, d)
            go_sibling(0, d)
            waiting["main"].append((0, d))
        if k == far:
            for d in offsets(far - 1) + offsets(far):
                go_x(1, d)

    last = 2 * far
    for k in range(1, last + 1):
        ready = {group: list(items) for group, items in waiting.items()}
        if k < far:
            partner_blocks(k)
        if k <= far:
            own_blocks(k)
        if far <= k <= far + 1:
            partner_blocks(k)
        if k == 1:
            from_x(2, 0)
            go_z(2, 0)
            go_sibling(2, 0)
            waiting["near"].append((2, 0))
        elif k <= far:
            for item, d in ring(k - 1):
                go_z(item, d)
        for item, d in ring(k):
            from_z(item, d)
            if k >= far:
                go_z(item, d)
            go_sibling(item, d)
            waiting["near"].append((item, d))
        straight = k - 1 if k < far else {last - 1: far - 1, last: far}.get(k)
        if straight is not None:
            for d in offsets(straight):
                from_x(1, d)
                go_sibling(4, d)
                waiting["main"].append((3, d))
        for kind in (0, 1):
            if 0 <= k - 1 - kind <= far:
                for d in offsets(k - 1 - kind):
                    from_cross(kind, d)
                    go_sibling(5 + kind, d)
                    waiting["guest"].append((5 + kind, d))
        if k == 1:
            settle(kept.at[pl.ds(0, tok_n - 1)], bulk_s.at[0])
            settle(kept.at[pl.ds(0, tok_n - 1)], bulk_r.at[0])
            factor_copy.wait()
            lax.fori_loop(0, tok_n, sign_rows, 0)
            for load in loads[7:]:
                load.wait()
        work(ready, 3)
    work({"main": [], "near": [], "guest": waiting["guest"]}, 1)
    work({"main": [], "near": waiting["near"], "guest": []}, 1)
    work({"main": waiting["main"], "near": [], "guest": []}, 1)

    row_factor = jnp.concatenate(
        [
            factor[0, :, pl.ds(pl.multiple_of(col * block, block), 2 * block)],
            factor[0, :, 3 * block :],
            factor[1, :, pl.ds(pl.multiple_of(give * block, block), block)],
        ],
        axis=1,
    )

    def activate(m, carry):
        gate = acc[pl.ds(pl.multiple_of(m * 64, 64), 64), :]
        up = acc[pl.ds(pl.multiple_of(units + m * 64, 64), 64), :]
        silu = gate / (1.0 + jnp.exp(-gate))
        hidden[pl.ds(pl.multiple_of(m * 64, 64), 64), :] = (row_factor * silu * up).astype(BF16)
        return carry

    lax.fori_loop(0, units // 64, activate, 0)

    strips = units // 128

    def packed(rows):
        tail = rows[:, strips * 128 :]
        tail = jnp.concatenate([tail[: kept_n // 2], tail[kept_n // 2 :]], axis=1)
        return jnp.concatenate([rows[:, c * 128 : (c + 1) * 128] for c in range(strips)] + [tail], axis=0)

    def unpacked(strip):
        blocks = [strip[c * kept_n : (c + 1) * kept_n, :] for c in range(strips)]
        tail = strip[strips * kept_n :, :]
        return jnp.concatenate(blocks + [jnp.concatenate([tail[:, :64], tail[:, 64:]], axis=0)], axis=1)

    owners_step = max(tok_n // 2, 1)
    for b in range(tok_n // owners_step):
        rows = slice(b * owners_step * kept_n, (b + 1) * owners_step * kept_n)
        product = lax.dot_general(
            table[rows, :], hidden[...], (((1,), (1,)), ((), ())), preferred_element_type=F32
        )
        for i in range(owners_step):
            part[b * owners_step + i] = packed(product[i * kept_n : (i + 1) * kept_n, :]).astype(BF16)

    for peer in tok_peers:
        pltpu.make_async_remote_copy(
            src_ref=part.at[peer], dst_ref=got.at[tok], send_sem=bulk_s.at[1], recv_sem=bulk_r.at[1],
            device_id={"tok": peer}, device_id_type=MESH,
        ).start()
    got[tok] = part[tok]
    settle(got.at[pl.ds(0, tok_n - 1)], bulk_r.at[1])
    total = got[0].astype(F32)
    for j in range(1, tok_n):
        total = total + got[j].astype(F32)
    mine = (total * row_scale).astype(BF16)
    sk[tok] = mine

    for peer in tok_peers:
        pltpu.make_async_remote_copy(
            src_ref=sk.at[tok], dst_ref=sk.at[tok], send_sem=bulk_s.at[2], recv_sem=bulk_r.at[2],
            device_id={"tok": peer}, device_id_type=MESH,
        ).start()
    settle(sk.at[pl.ds(0, tok_n - 1)], bulk_r.at[2])
    every = jnp.concatenate([unpacked(sk[j].astype(F32)).astype(BF16) for j in range(tok_n)], axis=0)
    gram = lax.dot_general(unpacked(mine.astype(F32)).astype(BF16), every, (((1,), (1,)), ((), ())), preferred_element_type=F32) * gram_scale

    tile_rows, tile_lanes = gs.shape[1:]
    across_n = gram.shape[1] // tile_lanes
    for t in range(hid_n):
        a, b = divmod(t, across_n)
        gs[t] = gram[a * tile_rows : (a + 1) * tile_rows, b * tile_lanes : (b + 1) * tile_lanes]

    for peer in hid_peers:
        pltpu.make_async_remote_copy(
            src_ref=gs.at[peer], dst_ref=gr.at[hid], send_sem=bulk_s.at[3], recv_sem=bulk_r.at[3],
            device_id={"hid": peer}, device_id_type=MESH,
        ).start()
    gr[hid] = gs[hid]
    settle(gr.at[pl.ds(0, hid_n - 1)], bulk_r.at[3])
    gf[hid] = jnp.sum(gr[...], axis=0)

    for peer in hid_peers:
        pltpu.make_async_remote_copy(
            src_ref=gf.at[hid], dst_ref=gf.at[hid], send_sem=bulk_s.at[4], recv_sem=bulk_r.at[4],
            device_id={"hid": peer}, device_id_type=MESH,
        ).start()
    for copy in sends:
        copy.wait_send()
    settle(part.at[pl.ds(0, tok_n - 1)], bulk_s.at[1])
    settle(sk.at[pl.ds(0, tok_n - 1)], bulk_s.at[2])
    settle(gs.at[pl.ds(0, hid_n - 1)], bulk_s.at[3])
    settle(gf.at[pl.ds(0, hid_n - 1)], bulk_r.at[4])
    for t in range(hid_n):
        a, b = divmod(t, across_n)
        out_ref[a * tile_rows : (a + 1) * tile_rows, b * tile_lanes : (b + 1) * tile_lanes] = gf[t]
    settle(gf.at[pl.ds(0, hid_n - 1)], bulk_s.at[4])


def per_device(tok_n, hid_n, activations, gate_weight, up_weight, row_signs, row_scales, kept_rows):
    tokens, width = activations.shape
    depth, units = gate_weight.shape
    kept_n = kept_rows.shape[0]
    zn = hid_n // 4
    far = zn // 2
    tile_lanes = kept_n * kept_n * tok_n // 8 // hid_n
    hbm = pl.BlockSpec(memory_space=pl.ANY)
    dma = pltpu.SemaphoreType.DMA
    return pl.pallas_call(
        functools.partial(fused, tok_n, hid_n, float(tokens * tok_n) ** -0.5, float(FF) ** -0.5),
        out_shape=jax.ShapeDtypeStruct((kept_n, kept_n * tok_n), F32),
        in_specs=[hbm] * 6,
        out_specs=pl.BlockSpec(memory_space=pltpu.VMEM),
        scratch_shapes=[
            pltpu.VMEM((hid_n // 2, 2, 4, tokens // 4, width), BF16),
            pltpu.VMEM((hid_n // 2, 2, tokens // 4, width), BF16),
            pltpu.VMEM((2 * units, depth), BF16),
            pltpu.VMEM((2 * units, tokens), F32),
            pltpu.VMEM((kept_n * tok_n, tokens), BF16),
            pltpu.VMEM((units, tokens), BF16),
            pltpu.VMEM((1, tokens), jnp.int32),
            pltpu.VMEM((1, tokens), F32),
            pltpu.VMEM((2, 1, tokens), F32),
            pltpu.VMEM((tok_n, 1, kept_n), jnp.int32),
            pltpu.VMEM((tok_n, kept_n * units // 128, 128), BF16),
            pltpu.VMEM((tok_n, kept_n * units // 128, 128), BF16),
            pltpu.VMEM((tok_n, kept_n * units // 128, 128), BF16),
            pltpu.VMEM((hid_n, 8, tile_lanes), F32),
            pltpu.VMEM((hid_n, 8, tile_lanes), F32),
            pltpu.VMEM((hid_n, 8, tile_lanes), F32),
            dma((9,)),
            dma((2, far, 3)),
            dma((2, far, 3)),
            dma((3, 2 * far)),
            dma((3, 2 * far)),
            dma((2, 2 * far)),
            dma((2, 2 * far)),
            dma((7, 2 * far)),
            dma((7, 2 * far)),
            dma((6,)),
            dma((6,)),
        ],
        compiler_params=pltpu.CompilerParams(
            collective_id=0, has_side_effects=True, vmem_limit_bytes=60 * 1024 * 1024
        ),
        name="sketch_gram",
    )(
        activations, gate_weight.T, up_weight.T,
        row_signs.reshape(1, -1), row_scales.reshape(1, -1), kept_rows.reshape(1, -1),
    )


def solution(mesh):
    placed = (P("tok", "hid"), P(None, "hid"), P(None, "hid"), P("tok"), P("tok"), P("tok"))
    return jax.shard_map(
        functools.partial(per_device, mesh.shape["tok"], mesh.shape["hid"]),
        mesh=mesh, in_specs=placed, out_specs=P("tok", None), check_vma=False,
    )
```

```python
import functools

import jax
import jax.numpy as jnp
from jax import lax
from jax.experimental import pallas as pl
from jax.experimental.pallas import tpu as pltpu
from jax.sharding import PartitionSpec as P

FF = 14336
MESH = pl.DeviceIdType.MESH
F32 = jnp.float32
BF16 = jnp.bfloat16


def bit_parity(value):
    for shift in (8, 4, 2, 1):
        value = value ^ (value >> shift)
    return value & 1


def diagonal_column(row, count):
    ids = lax.broadcasted_iota(jnp.int32, (count, count), 0)
    lanes = lax.broadcasted_iota(jnp.int32, (count, count), 1)
    spread = jnp.where(ids == lanes, jnp.broadcast_to(row, (count, count)), 0.0)
    return jnp.sum(spread, axis=1, keepdims=True)


def fused(
    tok_n, hid_n, row_scale, gram_scale,
    act_in, wg_in, wu_in, sgn_in, scl_in, kept_in, out_ref,
    act, guest, weights, acc, table, hidden, sgn, scl, factor, kept,
    part, got, sk, gs, gr, gf,
    load_sem, zs, zr, xs, xr, cs, cr, ss, sr, bulk_s, bulk_r,
):
    zn = hid_n // 4
    far = zn // 2
    tokens, width = act_in.shape
    block = tokens // 4
    depth = 2 * width
    kept_n = kept.shape[-1]
    units = wg_in.shape[0]
    tok = lax.axis_index("tok")
    hid = lax.axis_index("hid")
    core = lax.rem(hid, 2)
    here = lax.div(hid, 2)
    z = lax.rem(here, zn)
    col = lax.div(here, zn)
    way = 1 - 2 * core

    def chip(own, d):
        c = col if own else 1 - col
        return c * zn + lax.rem(z - d * way + 2 * zn, zn)

    def at_hid(q):
        return {"hid": q * 2 + core}

    ahead = at_hid(chip(True, -1))
    behind = at_hid(chip(True, 1))
    across = at_hid(chip(False, 0))
    sibling = {"hid": here * 2 + 1 - core}
    other_tok = tok + 1 - 2 * lax.rem(tok, 2)
    cross = {"tok": other_tok, "hid": chip(False, 0) * 2 + core}
    keep = 2 * col
    give = 2 - 2 * col

    def ring_order(n):
        return sorted(range(n), key=lambda step: -min(step, n - step))

    hid_peers = [
        (lax.rem(col + a, 2) * zn + lax.rem(z + step, zn)) * 2 + lax.rem(core + c, 2)
        for step in ring_order(zn) for a in (1, 0) for c in (1, 0) if step or a or c
    ]
    yn = tok_n // 2
    tok_peers = [
        lax.rem(lax.div(tok, 2) + step, yn) * 2 + lax.rem(tok + a, 2)
        for a in (1, 0) for step in ring_order(yn) if step or a
    ]

    loads = [
        pltpu.make_async_copy(act_in.at[pl.ds(b * block, block), :], act.at[here, core, b], load_sem.at[b])
        for b in range(4)
    ]
    loads += [
        pltpu.make_async_copy(src, dst, load_sem.at[4 + i])
        for i, (src, dst) in enumerate(((kept_in, kept.at[tok]), (sgn_in, sgn), (scl_in, scl),
                                         (wg_in, weights.at[pl.ds(0, units), :]), (wu_in, weights.at[pl.ds(units, units), :])))
    ]
    for load in loads:
        load.start()

    barrier = pltpu.get_barrier_semaphore()

    for peer in tok_peers:
        pl.semaphore_signal(barrier, inc=1, device_id={"tok": peer}, device_id_type=MESH)

    for neighbour in (ahead, behind, across, sibling, cross):
        pl.semaphore_signal(barrier, inc=1, device_id=neighbour, device_id_type=MESH)
    pl.semaphore_wait(barrier, 5 + tok_n - 1)

    sends = []

    def send(ref, send_sem, recv_sem, device, there=None):
        copy = pltpu.make_async_remote_copy(
            src_ref=ref, dst_ref=ref if there is None else there, send_sem=send_sem, recv_sem=recv_sem,
            device_id=device, device_id_type=MESH,
        )
        copy.start()
        sends.append(copy)

    def arrive(ref, send_sem, recv_sem):
        pltpu.make_async_remote_copy(
            src_ref=ref, dst_ref=ref, send_sem=send_sem, recv_sem=recv_sem, device_id=sibling, device_id_type=MESH
        ).wait_recv()

    def slot(d):
        return d if d >= 0 else far - d

    def z_piece(item, d):
        return act.at[chip(item < 4, d), core, (give, keep, 1, 3, 3)[item]]

    def go_z(item, d):
        if 0 <= d < far:
            send(z_piece(item, d), zs.at[0, d, item], zr.at[0, d, item], ahead)
        if -(far - 1) < d <= 0:
            send(z_piece(item, d), zs.at[1, -d, item], zr.at[1, -d, item], behind)

    def from_z(item, d):
        way_in = (0, d - 1) if d > 0 else (1, -d - 1)
        arrive(z_piece(item, d), zs.at[*way_in, item], zr.at[*way_in, item])

    def go_x(kind, d):
        b = (give, 1, 3)[kind]
        send(act.at[chip(True, d), core, b], xs.at[kind, slot(d)], xr.at[kind, slot(d)], across)

    def from_x(kind, d):
        b = (keep, 1, 3)[kind]
        arrive(act.at[chip(False, d), core, b], xs.at[kind, slot(d)], xr.at[kind, slot(d)])

    def go_cross(kind, d):
        q = chip(kind == 0, d)
        send(act.at[q, core, keep], cs.at[kind, slot(d)], cr.at[kind, slot(d)], cross, guest.at[q, core])

    def from_cross(kind, d):
        arrive(guest.at[chip(kind == 1, d), core], cs.at[kind, slot(d)], cr.at[kind, slot(d)])

    def shared(item, d, c):
        if item >= 5:
            return guest.at[chip(item == 6, d), c]
        shard = act.at[chip(item < 2, d), c]
        if item == 0:
            return shard.at[pl.ds(col, 2)]
        return shard.at[(None, 3, 3, keep, 1)[item]]

    def go_sibling(item, d):
        send(shared(item, d, core), ss.at[item, slot(d)], sr.at[item, slot(d)], sibling)

    def from_sibling(item, d):
        e = -d if abs(d) < far else d
        arrive(shared(item, d, 1 - core), ss.at[item, slot(e)], sr.at[item, slot(e)])

    def offsets(k):
        return [k] if k in (0, far) else [k, -k]

    def multiply(shards, read, start, first):
        left = jnp.concatenate(
            [weights[:, pl.ds(pl.multiple_of(q * depth, depth), depth)] for q in shards], axis=1
        )
        right = jnp.concatenate([read(q, c) for q in shards for c in range(2)], axis=1)
        product = lax.dot_general(left, right, (((1,), (1,)), ((), ())), preferred_element_type=F32)
        columns = pl.ds(start, block)
        acc[:, columns] = product if first else acc[:, columns] + product

    started = set()

    def jobs_of(group, items):
        shards = [chip(item in (0, 1, 6), d) for item, d in items]
        first = group not in started
        started.add(group)

        def come():
            for item, d in items:
                for part_item in (3, 4) if item == 3 else (item,):
                    from_sibling(part_item, d)

        if group == "near":
            return [lambda: (come(), multiply(shards, lambda q, c: act[q, c, 3], 2 * block, first))]
        if group == "guest":
            return [lambda: (come(), multiply(shards, lambda q, c: guest[q, c], 3 * block, first))]
        return [
            lambda: (come(), multiply(shards, lambda q, c: act[q, c, col], 0, first)),
            lambda: multiply(shards, lambda q, c: act[q, c, col + 1], block, first),
        ]

    def settle(ref, sem):
        pltpu.make_async_copy(ref, ref, sem).wait()

    for load in loads[:4]:
        load.wait()
    go_z(0, 0)
    go_x(2, 0)
    go_cross(0, 0)
    go_z(1, 0)
    go_x(0, 0)
    go_z(2, 0)
    go_z(3, 0)
    go_x(1, 0)
    go_sibling(0, 0)
    go_sibling(1, 0)
    for load in loads[4:7]:
        load.wait()
    for peer in tok_peers:
        pltpu.make_async_remote_copy(
            src_ref=kept.at[tok], dst_ref=kept.at[tok], send_sem=bulk_s.at[0], recv_sem=bulk_r.at[0],
            device_id={"tok": peer}, device_id_type=MESH,
        ).start()
    factor[0] = (2 * sgn[...] - 1).astype(F32) * scl[...]
    factor_copy = pltpu.make_async_remote_copy(
        src_ref=factor.at[0], dst_ref=factor.at[1], send_sem=bulk_s.at[5], recv_sem=bulk_r.at[5],
        device_id=cross, device_id_type=MESH,
    )
    factor_copy.start()

    spots = lax.broadcasted_iota(jnp.int32, (kept_n, tokens), 1)
    places = spots + jnp.where(spots < 2 * block, col * block, jnp.where(spots < 3 * block, block, (give - 3) * block))

    def sign_rows(j, carry):
        owner = jnp.where(spots < 3 * block, bit_parity(j & tok), bit_parity(j & other_tok))
        column = diagonal_column(kept[j].astype(F32), kept_n).astype(jnp.int32)
        parity = bit_parity(jnp.broadcast_to(column, (kept_n, tokens)) & places) ^ owner
        table[pl.ds(pl.multiple_of(j * kept_n, kept_n), kept_n), :] = (1 - 2 * parity).astype(F32).astype(BF16)
        return carry

    def ring(r):
        return [(3 + (r + 1) % 2, d) for d in offsets((r + 1) // 2)]

    waiting = {"main": [(0, 0)], "near": [(1, 0)], "guest": []}

    jobs = []

    def plan(group, items):
        jobs.extend(jobs_of(group, items))
        waiting[group] = waiting[group][len(items) :]

    def run(count):
        for job in jobs[:count]:
            job()
        del jobs[:count]

    def partner_blocks(k):
        for d in offsets(k - 1):
            from_x(0, d)
            go_cross(1, d)
            go_sibling(3, d)

    def own_blocks(k):
        for item in range(3):
            for d in offsets(k):
                from_z(item, d)
                go_z(item, d)
                if item == 0:
                    go_x(0, d)
                elif item == 1:
                    go_cross(0, d)
                else:
                    if k < far - 1:
                        go_x(1, d)
                    go_sibling(0, d)
                    waiting["main"].append((0, d))
        if k == far:
            for d in offsets(far - 1) + offsets(far):
                go_x(1, d)

    last = 2 * far
    for k in range(1, last + 1):
        for group in ("main", "near", "guest"):
            if len(waiting[group]) >= (3 if k < last else 1):
                plan(group, list(waiting[group]))
        if k < far:
            partner_blocks(k)
        if k <= far:
            own_blocks(k)
        if far <= k <= far + 1:
            partner_blocks(k)
        if k == 1:
            from_x(2, 0)
            go_z(4, 0)
            go_sibling(2, 0)
            waiting["near"].append((2, 0))
        elif k <= far:
            for item, d in ring(k - 1):
                go_z(item, d)
        run(len(jobs) if k >= last - 1 else 1)
        for item, d in ring(k):
            from_z(item, d)
            if k >= far:
                go_z(item, d)
            go_sibling(item - 2, d)
            waiting["near"].append((item - 2, d))
        straight = k - 1 if k < far else {last - 1: far - 1, last: far}.get(k)
        if straight is not None:
            for d in offsets(straight):
                from_x(1, d)
                go_sibling(4, d)
                waiting["main"].append((3, d))
        for kind in (0, 1):
            if 0 <= k - 1 - kind <= far:
                for d in offsets(k - 1 - kind):
                    from_cross(kind, d)
                    go_sibling(5 + kind, d)
                    waiting["guest"].append((5 + kind, d))
        if k == 1:
            settle(kept.at[pl.ds(0, tok_n - 1)], bulk_s.at[0])
            settle(kept.at[pl.ds(0, tok_n - 1)], bulk_r.at[0])
            factor_copy.wait()
            lax.fori_loop(0, tok_n, sign_rows, 0)
            for load in loads[7:]:
                load.wait()
        run(len(jobs))
    for group in ("guest", "near", "main"):
        if waiting[group]:
            plan(group, list(waiting[group]))
    run(len(jobs))

    row_factor = jnp.concatenate(
        [
            factor[0, :, pl.ds(pl.multiple_of(col * block, block), 2 * block)],
            factor[0, :, 3 * block :],
            factor[1, :, pl.ds(pl.multiple_of(give * block, block), block)],
        ],
        axis=1,
    )

    def activate(m, carry):
        gate = acc[pl.ds(pl.multiple_of(m * 64, 64), 64), :]
        up = acc[pl.ds(pl.multiple_of(units + m * 64, 64), 64), :]
        silu = gate / (1.0 + jnp.exp(-gate))
        hidden[pl.ds(pl.multiple_of(m * 64, 64), 64), :] = (row_factor * silu * up).astype(BF16)
        return carry

    lax.fori_loop(0, units // 64, activate, 0)

    strips = units // 128

    def packed(rows):
        tail = rows[:, strips * 128 :]
        tail = jnp.concatenate([tail[: kept_n // 2], tail[kept_n // 2 :]], axis=1)
        return jnp.concatenate([rows[:, c * 128 : (c + 1) * 128] for c in range(strips)] + [tail], axis=0)

    def unpacked(strip):
        blocks = [strip[c * kept_n : (c + 1) * kept_n, :] for c in range(strips)]
        tail = strip[strips * kept_n :, :]
        return jnp.concatenate(blocks + [jnp.concatenate([tail[:, :64], tail[:, 64:]], axis=0)], axis=1)

    owners_step = max(tok_n // 2, 1)
    for b in range(tok_n // owners_step):
        rows = slice(b * owners_step * kept_n, (b + 1) * owners_step * kept_n)
        product = lax.dot_general(
            table[rows, :], hidden[...], (((1,), (1,)), ((), ())), preferred_element_type=F32
        )
        for i in range(owners_step):
            part[b * owners_step + i] = packed(product[i * kept_n : (i + 1) * kept_n, :]).astype(BF16)

    for peer in tok_peers:
        pltpu.make_async_remote_copy(
            src_ref=part.at[peer], dst_ref=got.at[tok], send_sem=bulk_s.at[1], recv_sem=bulk_r.at[1],
            device_id={"tok": peer}, device_id_type=MESH,
        ).start()
    got[tok] = part[tok]
    settle(got.at[pl.ds(0, tok_n - 1)], bulk_r.at[1])
    total = got[0].astype(F32)
    for j in range(1, tok_n):
        total = total + got[j].astype(F32)
    mine = (total * row_scale).astype(BF16)
    sk[tok] = mine

    for peer in tok_peers:
        pltpu.make_async_remote_copy(
            src_ref=sk.at[tok], dst_ref=sk.at[tok], send_sem=bulk_s.at[2], recv_sem=bulk_r.at[2],
            device_id={"tok": peer}, device_id_type=MESH,
        ).start()
    settle(sk.at[pl.ds(0, tok_n - 1)], bulk_r.at[2])
    every = jnp.concatenate([unpacked(sk[j].astype(F32)).astype(BF16) for j in range(tok_n)], axis=0)
    gram = lax.dot_general(unpacked(mine.astype(F32)).astype(BF16), every, (((1,), (1,)), ((), ())), preferred_element_type=F32) * gram_scale

    tile_rows, tile_lanes = gs.shape[1:]
    across_n = gram.shape[1] // tile_lanes
    for t in range(hid_n):
        a, b = divmod(t, across_n)
        gs[t] = gram[a * tile_rows : (a + 1) * tile_rows, b * tile_lanes : (b + 1) * tile_lanes]

    for peer in hid_peers:
        pltpu.make_async_remote_copy(
            src_ref=gs.at[peer], dst_ref=gr.at[hid], send_sem=bulk_s.at[3], recv_sem=bulk_r.at[3],
            device_id={"hid": peer}, device_id_type=MESH,
        ).start()
    gr[hid] = gs[hid]
    settle(gr.at[pl.ds(0, hid_n - 1)], bulk_r.at[3])
    gf[hid] = jnp.sum(gr[...], axis=0)

    for peer in hid_peers:
        pltpu.make_async_remote_copy(
            src_ref=gf.at[hid], dst_ref=gf.at[hid], send_sem=bulk_s.at[4], recv_sem=bulk_r.at[4],
            device_id={"hid": peer}, device_id_type=MESH,
        ).start()
    for copy in sends:
        copy.wait_send()
    settle(part.at[pl.ds(0, tok_n - 1)], bulk_s.at[1])
    settle(sk.at[pl.ds(0, tok_n - 1)], bulk_s.at[2])
    settle(gs.at[pl.ds(0, hid_n - 1)], bulk_s.at[3])
    settle(gf.at[pl.ds(0, hid_n - 1)], bulk_r.at[4])
    for t in range(hid_n):
        a, b = divmod(t, across_n)
        out_ref[a * tile_rows : (a + 1) * tile_rows, b * tile_lanes : (b + 1) * tile_lanes] = gf[t]
    settle(gf.at[pl.ds(0, hid_n - 1)], bulk_s.at[4])


def per_device(tok_n, hid_n, activations, gate_weight, up_weight, row_signs, row_scales, kept_rows):
    tokens, width = activations.shape
    depth, units = gate_weight.shape
    kept_n = kept_rows.shape[0]
    zn = hid_n // 4
    far = zn // 2
    tile_lanes = kept_n * kept_n * tok_n // 8 // hid_n
    hbm = pl.BlockSpec(memory_space=pl.ANY)
    dma = pltpu.SemaphoreType.DMA
    return pl.pallas_call(
        functools.partial(fused, tok_n, hid_n, float(tokens * tok_n) ** -0.5, float(FF) ** -0.5),
        out_shape=jax.ShapeDtypeStruct((kept_n, kept_n * tok_n), F32),
        in_specs=[hbm] * 6,
        out_specs=pl.BlockSpec(memory_space=pltpu.VMEM),
        scratch_shapes=[
            pltpu.VMEM((hid_n // 2, 2, 4, tokens // 4, width), BF16),
            pltpu.VMEM((hid_n // 2, 2, tokens // 4, width), BF16),
            pltpu.VMEM((2 * units, depth), BF16),
            pltpu.VMEM((2 * units, tokens), F32),
            pltpu.VMEM((kept_n * tok_n, tokens), BF16),
            pltpu.VMEM((units, tokens), BF16),
            pltpu.VMEM((1, tokens), jnp.int32),
            pltpu.VMEM((1, tokens), F32),
            pltpu.VMEM((2, 1, tokens), F32),
            pltpu.VMEM((tok_n, 1, kept_n), jnp.int32),
            pltpu.VMEM((tok_n, kept_n * units // 128, 128), BF16),
            pltpu.VMEM((tok_n, kept_n * units // 128, 128), BF16),
            pltpu.VMEM((tok_n, kept_n * units // 128, 128), BF16),
            pltpu.VMEM((hid_n, 8, tile_lanes), F32),
            pltpu.VMEM((hid_n, 8, tile_lanes), F32),
            pltpu.VMEM((hid_n, 8, tile_lanes), F32),
            dma((9,)),
            dma((2, far, 5)),
            dma((2, far, 5)),
            dma((3, 2 * far)),
            dma((3, 2 * far)),
            dma((2, 2 * far)),
            dma((2, 2 * far)),
            dma((7, 2 * far)),
            dma((7, 2 * far)),
            dma((6,)),
            dma((6,)),
        ],
        compiler_params=pltpu.CompilerParams(
            collective_id=0, has_side_effects=True, vmem_limit_bytes=60 * 1024 * 1024
        ),
        name="sketch_gram",
    )(
        activations, gate_weight.T, up_weight.T,
        row_signs.reshape(1, -1), row_scales.reshape(1, -1), kept_rows.reshape(1, -1),
    )


def solution(mesh):
    placed = (P("tok", "hid"), P(None, "hid"), P(None, "hid"), P("tok"), P("tok"), P("tok"))
    return jax.shard_map(
        functools.partial(per_device, mesh.shape["tok"], mesh.shape["hid"]),
        mesh=mesh, in_specs=placed, out_specs=P("tok", None), check_vma=False,
    )
```

```python
import functools

import jax
import jax.numpy as jnp
from jax import lax
from jax.experimental import pallas as pl
from jax.experimental.pallas import tpu as pltpu
from jax.sharding import PartitionSpec as P

FF = 14336
MESH = pl.DeviceIdType.MESH
F32 = jnp.float32
BF16 = jnp.bfloat16


def bit_parity(value):
    for shift in (8, 4, 2, 1):
        value = value ^ (value >> shift)
    return value & 1


def diagonal_column(row, count):
    ids = lax.broadcasted_iota(jnp.int32, (count, count), 0)
    lanes = lax.broadcasted_iota(jnp.int32, (count, count), 1)
    spread = jnp.where(ids == lanes, jnp.broadcast_to(row, (count, count)), 0.0)
    return jnp.sum(spread, axis=1, keepdims=True)


def fused(
    tok_n, hid_n, row_scale, gram_scale,
    act_in, wg_in, wu_in, sgn_in, scl_in, kept_in, out_ref,
    act, guest, weights, acc, table, hidden, sgn, scl, factor, kept,
    part, got, sk, gs, gr, gf,
    load_sem, zs, zr, xs, xr, cs, cr, ss, sr, bulk_s, bulk_r,
):
    zn = hid_n // 4
    far = zn // 2
    tokens, width = act_in.shape
    block = tokens // 4
    depth = 2 * width
    kept_n = kept.shape[-1]
    units = wg_in.shape[0]
    tok = lax.axis_index("tok")
    hid = lax.axis_index("hid")
    core = lax.rem(hid, 2)
    here = lax.div(hid, 2)
    z = lax.rem(here, zn)
    col = lax.div(here, zn)
    way = 1 - 2 * core

    def chip(own, d):
        c = col if own else 1 - col
        return c * zn + lax.rem(z - d * way + 2 * zn, zn)

    def at_hid(q):
        return {"hid": q * 2 + core}

    ahead = at_hid(chip(True, -1))
    behind = at_hid(chip(True, 1))
    across = at_hid(chip(False, 0))
    sibling = {"hid": here * 2 + 1 - core}
    other_tok = tok + 1 - 2 * lax.rem(tok, 2)
    cross = {"tok": other_tok, "hid": chip(False, 0) * 2 + core}
    keep = 2 * col
    give = 2 - 2 * col

    def ring_order(n):
        return sorted(range(n), key=lambda step: -min(step, n - step))

    hid_peers = [
        (lax.rem(col + a, 2) * zn + lax.rem(z + step, zn)) * 2 + lax.rem(core + c, 2)
        for step in ring_order(zn) for a in (1, 0) for c in (1, 0) if step or a or c
    ]
    yn = tok_n // 2
    tok_peers = [
        lax.rem(lax.div(tok, 2) + step, yn) * 2 + lax.rem(tok + a, 2)
        for a in (1, 0) for step in ring_order(yn) if step or a
    ]

    loads = [
        pltpu.make_async_copy(act_in.at[pl.ds(b * block, block), :], act.at[here, core, b], load_sem.at[b])
        for b in range(4)
    ]
    loads += [
        pltpu.make_async_copy(src, dst, load_sem.at[4 + i])
        for i, (src, dst) in enumerate(((kept_in, kept.at[tok]), (sgn_in, sgn), (scl_in, scl),
                                         (wg_in, weights.at[pl.ds(0, units), :]), (wu_in, weights.at[pl.ds(units, units), :])))
    ]
    for load in loads:
        load.start()

    barrier = pltpu.get_barrier_semaphore()

    for peer in tok_peers:
        pl.semaphore_signal(barrier, inc=1, device_id={"tok": peer}, device_id_type=MESH)

    for neighbour in (ahead, behind, across, sibling, cross):
        pl.semaphore_signal(barrier, inc=1, device_id=neighbour, device_id_type=MESH)
    pl.semaphore_wait(barrier, 5 + tok_n - 1)

    sends = []

    def send(ref, send_sem, recv_sem, device, there=None):
        copy = pltpu.make_async_remote_copy(
            src_ref=ref, dst_ref=ref if there is None else there, send_sem=send_sem, recv_sem=recv_sem,
            device_id=device, device_id_type=MESH,
        )
        copy.start()
        sends.append(copy)

    def arrive(ref, send_sem, recv_sem):
        pltpu.make_async_remote_copy(
            src_ref=ref, dst_ref=ref, send_sem=send_sem, recv_sem=recv_sem, device_id=sibling, device_id_type=MESH
        ).wait_recv()

    def slot(d):
        return d if d >= 0 else far - d

    def z_piece(item, d):
        return act.at[chip(item < 4, d), core, (give, keep, 1, 3, 3)[item]]

    def go_z(item, d):
        if 0 <= d < far:
            send(z_piece(item, d), zs.at[0, d, item], zr.at[0, d, item], ahead)
        if -(far - 1) < d <= 0:
            send(z_piece(item, d), zs.at[1, -d, item], zr.at[1, -d, item], behind)

    def from_z(item, d):
        way_in = (0, d - 1) if d > 0 else (1, -d - 1)
        arrive(z_piece(item, d), zs.at[*way_in, item], zr.at[*way_in, item])

    def go_x(kind, d):
        b = (give, 1, 3)[kind]
        send(act.at[chip(True, d), core, b], xs.at[kind, slot(d)], xr.at[kind, slot(d)], across)

    def from_x(kind, d):
        b = (keep, 1, 3)[kind]
        arrive(act.at[chip(False, d), core, b], xs.at[kind, slot(d)], xr.at[kind, slot(d)])

    def go_cross(kind, d):
        q = chip(kind == 0, d)
        send(act.at[q, core, keep], cs.at[kind, slot(d)], cr.at[kind, slot(d)], cross, guest.at[q, core])

    def from_cross(kind, d):
        arrive(guest.at[chip(kind == 1, d), core], cs.at[kind, slot(d)], cr.at[kind, slot(d)])

    def shared(item, d, c):
        if item >= 5:
            return guest.at[chip(item == 6, d), c]
        shard = act.at[chip(item < 2, d), c]
        if item == 0:
            return shard.at[pl.ds(col, 2)]
        return shard.at[(None, 3, 3, keep, 1)[item]]

    def go_sibling(item, d):
        send(shared(item, d, core), ss.at[item, slot(d)], sr.at[item, slot(d)], sibling)

    def from_sibling(item, d):
        e = -d if abs(d) < far else d
        arrive(shared(item, d, 1 - core), ss.at[item, slot(e)], sr.at[item, slot(e)])

    def offsets(k):
        return [k] if k in (0, far) else [k, -k]

    def multiply(shards, read, start, first):
        left = jnp.concatenate(
            [weights[:, pl.ds(pl.multiple_of(q * depth, depth), depth)] for q in shards], axis=1
        )
        right = jnp.concatenate([read(q, c) for q in shards for c in range(2)], axis=1)
        product = lax.dot_general(left, right, (((1,), (1,)), ((), ())), preferred_element_type=F32)
        columns = pl.ds(start, block)
        acc[:, columns] = product if first else acc[:, columns] + product

    started = set()

    def jobs_of(group, items):
        shards = [chip(item in (0, 1, 6), d) for item, d in items]
        first = group not in started
        started.add(group)

        def come():
            for item, d in items:
                for part_item in (3, 4) if item == 3 else (item,):
                    from_sibling(part_item, d)

        if group == "near":
            return [lambda: (come(), multiply(shards, lambda q, c: act[q, c, 3], 2 * block, first))]
        if group == "guest":
            return [lambda: (come(), multiply(shards, lambda q, c: guest[q, c], 3 * block, first))]

        def tile(m, carry):
            multiply(shards, lambda q, c: act[q, c, col + m], pl.multiple_of(m * block, block), first)
            return carry

        return [lambda: (come(), lax.fori_loop(0, 2, tile, 0))]

    def settle(ref, sem):
        pltpu.make_async_copy(ref, ref, sem).wait()

    for load in loads[:4]:
        load.wait()
    go_z(0, 0)
    go_x(2, 0)
    go_cross(0, 0)
    go_z(1, 0)
    go_x(0, 0)
    go_z(2, 0)
    go_z(3, 0)
    go_x(1, 0)
    go_sibling(0, 0)
    go_sibling(1, 0)
    for load in loads[4:7]:
        load.wait()
    for peer in tok_peers:
        pltpu.make_async_remote_copy(
            src_ref=kept.at[tok], dst_ref=kept.at[tok], send_sem=bulk_s.at[0], recv_sem=bulk_r.at[0],
            device_id={"tok": peer}, device_id_type=MESH,
        ).start()
    factor[0] = (2 * sgn[...] - 1).astype(F32) * scl[...]
    factor_copy = pltpu.make_async_remote_copy(
        src_ref=factor.at[0], dst_ref=factor.at[1], send_sem=bulk_s.at[5], recv_sem=bulk_r.at[5],
        device_id=cross, device_id_type=MESH,
    )
    factor_copy.start()

    spots = lax.broadcasted_iota(jnp.int32, (kept_n, tokens), 1)
    places = spots + jnp.where(spots < 2 * block, col * block, jnp.where(spots < 3 * block, block, (give - 3) * block))

    def sign_rows(j, carry):
        owner = jnp.where(spots < 3 * block, bit_parity(j & tok), bit_parity(j & other_tok))
        column = diagonal_column(kept[j].astype(F32), kept_n).astype(jnp.int32)
        parity = bit_parity(jnp.broadcast_to(column, (kept_n, tokens)) & places) ^ owner
        table[pl.ds(pl.multiple_of(j * kept_n, kept_n), kept_n), :] = (1 - 2 * parity).astype(F32).astype(BF16)
        return carry

    def ring(r):
        return [(3 + (r + 1) % 2, d) for d in offsets((r + 1) // 2)]

    waiting = {"main": [(0, 0)], "near": [(1, 0)], "guest": []}

    jobs = []

    def plan(group, items):
        jobs.extend(jobs_of(group, items))
        waiting[group] = waiting[group][len(items) :]

    def run(count):
        for job in jobs[:count]:
            job()
        del jobs[:count]

    def partner_blocks(k):
        for d in offsets(k - 1):
            from_x(0, d)
            go_cross(1, d)
            go_sibling(3, d)

    def own_blocks(k):
        for item in range(3):
            for d in offsets(k):
                from_z(item, d)
                go_z(item, d)
                if item == 0:
                    go_x(0, d)
                elif item == 1:
                    go_cross(0, d)
                else:
                    go_x(1, d)
                    go_sibling(0, d)
                    waiting["main"].append((0, d))

    last = 2 * far
    for k in range(1, last + 1):
        for group in ("main", "near", "guest"):
            if len(waiting[group]) >= (3 if k < last else 1):
                plan(group, list(waiting[group]))
        if k < far:
            partner_blocks(k)
        if k <= far:
            own_blocks(k)
        if far <= k <= far + 1:
            partner_blocks(k)
        if k == 1:
            from_x(2, 0)
            go_z(4, 0)
            go_sibling(2, 0)
            waiting["near"].append((2, 0))
        elif k <= far:
            for item, d in ring(k - 1):
                go_z(item, d)
        run(len(jobs) if k >= last - 1 else 1)
        for item, d in ring(k):
            from_z(item, d)
            if k >= far:
                go_z(item, d)
            go_sibling(item - 2, d)
            waiting["near"].append((item - 2, d))
        straight = k - 1 if k <= far + 1 else None
        if straight is not None:
            for d in offsets(straight):
                from_x(1, d)
                go_sibling(4, d)
                waiting["main"].append((3, d))
        for kind in (0, 1):
            if 0 <= k - 1 - kind <= far:
                for d in offsets(k - 1 - kind):
                    from_cross(kind, d)
                    go_sibling(5 + kind, d)
                    waiting["guest"].append((5 + kind, d))
        if k == 1:
            settle(kept.at[pl.ds(0, tok_n - 1)], bulk_s.at[0])
            settle(kept.at[pl.ds(0, tok_n - 1)], bulk_r.at[0])
            factor_copy.wait()
            lax.fori_loop(0, tok_n, sign_rows, 0)
            for load in loads[7:]:
                load.wait()
        run(len(jobs))
    for group in ("guest", "near", "main"):
        if waiting[group]:
            plan(group, list(waiting[group]))
    run(len(jobs))

    row_factor = jnp.concatenate(
        [
            factor[0, :, pl.ds(pl.multiple_of(col * block, block), 2 * block)],
            factor[0, :, 3 * block :],
            factor[1, :, pl.ds(pl.multiple_of(give * block, block), block)],
        ],
        axis=1,
    )

    def activate(m, carry):
        gate = acc[pl.ds(pl.multiple_of(m * 64, 64), 64), :]
        up = acc[pl.ds(pl.multiple_of(units + m * 64, 64), 64), :]
        silu = gate / (1.0 + jnp.exp(-gate))
        hidden[pl.ds(pl.multiple_of(m * 64, 64), 64), :] = (row_factor * silu * up).astype(BF16)
        return carry

    lax.fori_loop(0, units // 64, activate, 0)

    strips = units // 128

    def packed(rows):
        tail = rows[:, strips * 128 :]
        tail = jnp.concatenate([tail[: kept_n // 2], tail[kept_n // 2 :]], axis=1)
        return jnp.concatenate([rows[:, c * 128 : (c + 1) * 128] for c in range(strips)] + [tail], axis=0)

    def unpacked(strip):
        blocks = [strip[c * kept_n : (c + 1) * kept_n, :] for c in range(strips)]
        tail = strip[strips * kept_n :, :]
        return jnp.concatenate(blocks + [jnp.concatenate([tail[:, :64], tail[:, 64:]], axis=0)], axis=1)

    owners_step = max(tok_n // 2, 1)
    for b in range(tok_n // owners_step):
        rows = slice(b * owners_step * kept_n, (b + 1) * owners_step * kept_n)
        product = lax.dot_general(
            table[rows, :], hidden[...], (((1,), (1,)), ((), ())), preferred_element_type=F32
        )
        for i in range(owners_step):
            part[b * owners_step + i] = packed(product[i * kept_n : (i + 1) * kept_n, :]).astype(BF16)

    for peer in tok_peers:
        pltpu.make_async_remote_copy(
            src_ref=part.at[peer], dst_ref=got.at[tok], send_sem=bulk_s.at[1], recv_sem=bulk_r.at[1],
            device_id={"tok": peer}, device_id_type=MESH,
        ).start()
    got[tok] = part[tok]
    settle(got.at[pl.ds(0, tok_n - 1)], bulk_r.at[1])
    total = got[0].astype(F32)
    for j in range(1, tok_n):
        total = total + got[j].astype(F32)
    mine = (total * row_scale).astype(BF16)
    sk[tok] = mine

    for peer in tok_peers:
        pltpu.make_async_remote_copy(
            src_ref=sk.at[tok], dst_ref=sk.at[tok], send_sem=bulk_s.at[2], recv_sem=bulk_r.at[2],
            device_id={"tok": peer}, device_id_type=MESH,
        ).start()
    settle(sk.at[pl.ds(0, tok_n - 1)], bulk_r.at[2])
    every = jnp.concatenate([unpacked(sk[j].astype(F32)).astype(BF16) for j in range(tok_n)], axis=0)
    gram = lax.dot_general(unpacked(mine.astype(F32)).astype(BF16), every, (((1,), (1,)), ((), ())), preferred_element_type=F32) * gram_scale

    tile_rows, tile_lanes = gs.shape[1:]
    across_n = gram.shape[1] // tile_lanes
    for t in range(hid_n):
        a, b = divmod(t, across_n)
        gs[t] = gram[a * tile_rows : (a + 1) * tile_rows, b * tile_lanes : (b + 1) * tile_lanes]

    for peer in hid_peers:
        pltpu.make_async_remote_copy(
            src_ref=gs.at[peer], dst_ref=gr.at[hid], send_sem=bulk_s.at[3], recv_sem=bulk_r.at[3],
            device_id={"hid": peer}, device_id_type=MESH,
        ).start()
    gr[hid] = gs[hid]
    settle(gr.at[pl.ds(0, hid_n - 1)], bulk_r.at[3])
    gf[hid] = jnp.sum(gr[...], axis=0)

    for peer in hid_peers:
        pltpu.make_async_remote_copy(
            src_ref=gf.at[hid], dst_ref=gf.at[hid], send_sem=bulk_s.at[4], recv_sem=bulk_r.at[4],
            device_id={"hid": peer}, device_id_type=MESH,
        ).start()
    for copy in sends:
        copy.wait_send()
    settle(part.at[pl.ds(0, tok_n - 1)], bulk_s.at[1])
    settle(sk.at[pl.ds(0, tok_n - 1)], bulk_s.at[2])
    settle(gs.at[pl.ds(0, hid_n - 1)], bulk_s.at[3])
    settle(gf.at[pl.ds(0, hid_n - 1)], bulk_r.at[4])
    for t in range(hid_n):
        a, b = divmod(t, across_n)
        out_ref[a * tile_rows : (a + 1) * tile_rows, b * tile_lanes : (b + 1) * tile_lanes] = gf[t]
    settle(gf.at[pl.ds(0, hid_n - 1)], bulk_s.at[4])


def per_device(tok_n, hid_n, activations, gate_weight, up_weight, row_signs, row_scales, kept_rows):
    tokens, width = activations.shape
    depth, units = gate_weight.shape
    kept_n = kept_rows.shape[0]
    zn = hid_n // 4
    far = zn // 2
    tile_lanes = kept_n * kept_n * tok_n // 8 // hid_n
    hbm = pl.BlockSpec(memory_space=pl.ANY)
    dma = pltpu.SemaphoreType.DMA
    return pl.pallas_call(
        functools.partial(fused, tok_n, hid_n, float(tokens * tok_n) ** -0.5, float(FF) ** -0.5),
        out_shape=jax.ShapeDtypeStruct((kept_n, kept_n * tok_n), F32),
        in_specs=[hbm] * 6,
        out_specs=pl.BlockSpec(memory_space=pltpu.VMEM),
        scratch_shapes=[
            pltpu.VMEM((hid_n // 2, 2, 4, tokens // 4, width), BF16),
            pltpu.VMEM((hid_n // 2, 2, tokens // 4, width), BF16),
            pltpu.VMEM((2 * units, depth), BF16),
            pltpu.VMEM((2 * units, tokens), F32),
            pltpu.VMEM((kept_n * tok_n, tokens), BF16),
            pltpu.VMEM((units, tokens), BF16),
            pltpu.VMEM((1, tokens), jnp.int32),
            pltpu.VMEM((1, tokens), F32),
            pltpu.VMEM((2, 1, tokens), F32),
            pltpu.VMEM((tok_n, 1, kept_n), jnp.int32),
            pltpu.VMEM((tok_n, kept_n * units // 128, 128), BF16),
            pltpu.VMEM((tok_n, kept_n * units // 128, 128), BF16),
            pltpu.VMEM((tok_n, kept_n * units // 128, 128), BF16),
            pltpu.VMEM((hid_n, 8, tile_lanes), F32),
            pltpu.VMEM((hid_n, 8, tile_lanes), F32),
            pltpu.VMEM((hid_n, 8, tile_lanes), F32),
            dma((9,)),
            dma((2, far, 5)),
            dma((2, far, 5)),
            dma((3, 2 * far)),
            dma((3, 2 * far)),
            dma((2, 2 * far)),
            dma((2, 2 * far)),
            dma((7, 2 * far)),
            dma((7, 2 * far)),
            dma((6,)),
            dma((6,)),
        ],
        compiler_params=pltpu.CompilerParams(
            collective_id=0, has_side_effects=True, vmem_limit_bytes=60 * 1024 * 1024
        ),
        name="sketch_gram",
    )(
        activations, gate_weight.T, up_weight.T,
        row_signs.reshape(1, -1), row_scales.reshape(1, -1), kept_rows.reshape(1, -1),
    )


def solution(mesh):
    placed = (P("tok", "hid"), P(None, "hid"), P(None, "hid"), P("tok"), P("tok"), P("tok"))
    return jax.shard_map(
        functools.partial(per_device, mesh.shape["tok"], mesh.shape["hid"]),
        mesh=mesh, in_specs=placed, out_specs=P("tok", None), check_vma=False,
    )
```

```python
import functools

import jax
import jax.numpy as jnp
from jax import lax
from jax.experimental import pallas as pl
from jax.experimental.pallas import tpu as pltpu
from jax.sharding import PartitionSpec as P

FF = 14336
MESH = pl.DeviceIdType.MESH
F32 = jnp.float32
BF16 = jnp.bfloat16


def bit_parity(value):
    for shift in (8, 4, 2, 1):
        value = value ^ (value >> shift)
    return value & 1


def diagonal_column(row, count):
    ids = lax.broadcasted_iota(jnp.int32, (count, count), 0)
    lanes = lax.broadcasted_iota(jnp.int32, (count, count), 1)
    spread = jnp.where(ids == lanes, jnp.broadcast_to(row, (count, count)), 0.0)
    return jnp.sum(spread, axis=1, keepdims=True)


def fused(
    tok_n, hid_n, row_scale, gram_scale,
    act_in, wg_in, wu_in, sgn_in, scl_in, kept_in, out_ref,
    act, guest, weights, acc, table, hidden, sgn, scl, factor, kept,
    part, got, sk, gs, gr, gf,
    load_sem, zs, zr, xs, xr, cs, cr, ss, sr, bulk_s, bulk_r,
):
    zn = hid_n // 4
    far = zn // 2
    tokens, width = act_in.shape
    block = tokens // 4
    depth = 2 * width
    kept_n = kept.shape[-1]
    units = wg_in.shape[0]
    tok = lax.axis_index("tok")
    hid = lax.axis_index("hid")
    core = lax.rem(hid, 2)
    here = lax.div(hid, 2)
    z = lax.rem(here, zn)
    col = lax.div(here, zn)
    way = 1 - 2 * core

    def chip(own, d):
        c = col if own else 1 - col
        return c * zn + lax.rem(z - d * way + 2 * zn, zn)

    def at_hid(q):
        return {"hid": q * 2 + core}

    ahead = at_hid(chip(True, -1))
    behind = at_hid(chip(True, 1))
    across = at_hid(chip(False, 0))
    sibling = {"hid": here * 2 + 1 - core}
    other_tok = tok + 1 - 2 * lax.rem(tok, 2)
    cross = {"tok": other_tok, "hid": chip(False, 0) * 2 + core}
    keep = 2 * col
    give = 2 - 2 * col

    def ring_order(n):
        return sorted(range(n), key=lambda step: -min(step, n - step))

    def to_hid_peers(start_copy):
        def start_four(step, skip_self):
            for a in (1, 0):
                for c in (1, 0):
                    if a or c or not skip_self:
                        shard = lax.rem(col + a, 2) * zn + lax.rem(z + step, zn)
                        start_copy(shard * 2 + lax.rem(core + c, 2))

        def ring_step(i, carry):
            start_four(far + (1 - 2 * lax.rem(i, 2)) * lax.div(i + 1, 2), False)
            return carry

        lax.fori_loop(0, zn - 1, ring_step, 0)
        start_four(0, True)

    yn = tok_n // 2
    tok_peers = [
        lax.rem(lax.div(tok, 2) + step, yn) * 2 + lax.rem(tok + a, 2)
        for a in (1, 0) for step in ring_order(yn) if step or a
    ]

    loads = [
        pltpu.make_async_copy(act_in.at[pl.ds(b * block, block), :], act.at[here, core, b], load_sem.at[b])
        for b in range(4)
    ]
    loads += [
        pltpu.make_async_copy(src, dst, load_sem.at[4 + i])
        for i, (src, dst) in enumerate(((kept_in, kept.at[tok]), (sgn_in, sgn), (scl_in, scl),
                                         (wg_in, weights.at[pl.ds(0, units), :]), (wu_in, weights.at[pl.ds(units, units), :])))
    ]
    for load in loads:
        load.start()

    barrier = pltpu.get_barrier_semaphore()

    for peer in tok_peers:
        pl.semaphore_signal(barrier, inc=1, device_id={"tok": peer}, device_id_type=MESH)

    for neighbour in (ahead, behind, across, sibling, cross):
        pl.semaphore_signal(barrier, inc=1, device_id=neighbour, device_id_type=MESH)
    pl.semaphore_wait(barrier, 5 + tok_n - 1)

    sends = []

    def send(ref, send_sem, recv_sem, device, there=None):
        copy = pltpu.make_async_remote_copy(
            src_ref=ref, dst_ref=ref if there is None else there, send_sem=send_sem, recv_sem=recv_sem,
            device_id=device, device_id_type=MESH,
        )
        copy.start()
        sends.append(copy)

    def arrive(ref, send_sem, recv_sem):
        pltpu.make_async_remote_copy(
            src_ref=ref, dst_ref=ref, send_sem=send_sem, recv_sem=recv_sem, device_id=sibling, device_id_type=MESH
        ).wait_recv()

    def slot(d):
        return d if d >= 0 else far - d

    def z_piece(item, d):
        return act.at[chip(item < 4, d), core, (give, keep, 1, 3, 3)[item]]

    def go_z(item, d):
        if 0 <= d < far:
            send(z_piece(item, d), zs.at[0, d, item], zr.at[0, d, item], ahead)
        if -(far - 1) < d <= 0:
            send(z_piece(item, d), zs.at[1, -d, item], zr.at[1, -d, item], behind)

    def from_z(item, d):
        way_in = (0, d - 1) if d > 0 else (1, -d - 1)
        arrive(z_piece(item, d), zs.at[*way_in, item], zr.at[*way_in, item])

    def go_x(kind, d):
        b = (give, 1, 3)[kind]
        send(act.at[chip(True, d), core, b], xs.at[kind, slot(d)], xr.at[kind, slot(d)], across)

    def from_x(kind, d):
        b = (keep, 1, 3)[kind]
        arrive(act.at[chip(False, d), core, b], xs.at[kind, slot(d)], xr.at[kind, slot(d)])

    def go_cross(kind, d):
        q = chip(kind == 0, d)
        send(act.at[q, core, keep], cs.at[kind, slot(d)], cr.at[kind, slot(d)], cross, guest.at[q, core])

    def from_cross(kind, d):
        arrive(guest.at[chip(kind == 1, d), core], cs.at[kind, slot(d)], cr.at[kind, slot(d)])

    def shared(item, d, c):
        if item >= 5:
            return guest.at[chip(item == 6, d), c]
        shard = act.at[chip(item < 2, d), c]
        if item == 0:
            return shard.at[pl.ds(col, 2)]
        return shard.at[(None, 3, 3, keep, 1)[item]]

    def go_sibling(item, d):
        send(shared(item, d, core), ss.at[item, slot(d)], sr.at[item, slot(d)], sibling)

    def from_sibling(item, d):
        e = -d if abs(d) < far else d
        arrive(shared(item, d, 1 - core), ss.at[item, slot(e)], sr.at[item, slot(e)])

    def offsets(k):
        return [k] if k in (0, far) else [k, -k]

    def multiply(shards, read, start, first):
        left = jnp.concatenate(
            [weights[:, pl.ds(pl.multiple_of(q * depth, depth), depth)] for q in shards], axis=1
        )
        right = jnp.concatenate([read(q, c) for q in shards for c in range(2)], axis=1)
        product = lax.dot_general(left, right, (((1,), (1,)), ((), ())), preferred_element_type=F32)
        columns = pl.ds(start, block)
        acc[:, columns] = product if first else acc[:, columns] + product

    started = set()

    def jobs_of(group, items):
        shards = [chip(item in (0, 1, 6), d) for item, d in items]
        first = group not in started
        started.add(group)

        def come():
            for item, d in items:
                for part_item in (3, 4) if item == 3 else (item,):
                    from_sibling(part_item, d)

        if group == "near":
            return [lambda: (come(), multiply(shards, lambda q, c: act[q, c, 3], 2 * block, first))]
        if group == "guest":
            return [lambda: (come(), multiply(shards, lambda q, c: guest[q, c], 3 * block, first))]

        def tile(m, carry):
            multiply(shards, lambda q, c: act[q, c, col + m], pl.multiple_of(m * block, block), first)
            return carry

        return [lambda: (come(), lax.fori_loop(0, 2, tile, 0))]

    def settle(ref, sem):
        pltpu.make_async_copy(ref, ref, sem).wait()

    for load in loads[:4]:
        load.wait()
    go_z(0, 0)
    go_x(2, 0)
    go_cross(0, 0)
    go_z(1, 0)
    go_x(0, 0)
    go_z(2, 0)
    go_z(3, 0)
    go_x(1, 0)
    go_sibling(0, 0)
    go_sibling(1, 0)
    for load in loads[4:7]:
        load.wait()
    for peer in tok_peers:
        pltpu.make_async_remote_copy(
            src_ref=kept.at[tok], dst_ref=kept.at[tok], send_sem=bulk_s.at[0], recv_sem=bulk_r.at[0],
            device_id={"tok": peer}, device_id_type=MESH,
        ).start()
    factor[0] = (2 * sgn[...] - 1).astype(F32) * scl[...]
    factor_copy = pltpu.make_async_remote_copy(
        src_ref=factor.at[0], dst_ref=factor.at[1], send_sem=bulk_s.at[5], recv_sem=bulk_r.at[5],
        device_id=cross, device_id_type=MESH,
    )
    factor_copy.start()

    spots = lax.broadcasted_iota(jnp.int32, (kept_n, tokens), 1)
    places = spots + jnp.where(spots < 2 * block, col * block, jnp.where(spots < 3 * block, block, (give - 3) * block))

    def sign_rows(j, carry):
        owner = jnp.where(spots < 3 * block, bit_parity(j & tok), bit_parity(j & other_tok))
        column = diagonal_column(kept[j].astype(F32), kept_n).astype(jnp.int32)
        parity = bit_parity(jnp.broadcast_to(column, (kept_n, tokens)) & places) ^ owner
        table[pl.ds(pl.multiple_of(j * kept_n, kept_n), kept_n), :] = (1 - 2 * parity).astype(F32).astype(BF16)
        return carry

    def ring(r):
        return [(3 + (r + 1) % 2, d) for d in offsets((r + 1) // 2)]

    waiting = {"main": [(0, 0)], "near": [(1, 0)], "guest": []}

    jobs = []

    def plan(group, items):
        jobs.extend(jobs_of(group, items))
        waiting[group] = waiting[group][len(items) :]

    def run(count):
        for job in jobs[:count]:
            job()
        del jobs[:count]

    def partner_blocks(k):
        for d in offsets(k - 1):
            from_x(0, d)
            go_cross(1, d)
            go_sibling(3, d)

    def own_blocks(k):
        for item in range(3):
            for d in offsets(k):
                from_z(item, d)
                go_z(item, d)
                if item == 0:
                    go_x(0, d)
                elif item == 1:
                    go_cross(0, d)
                else:
                    go_x(1, d)
                    go_sibling(0, d)
                    waiting["main"].append((0, d))

    last = 2 * far
    for k in range(1, last + 1):
        for group in ("main", "near", "guest"):
            if len(waiting[group]) >= (3 if k < last else 1):
                plan(group, list(waiting[group]))
        if k < far:
            partner_blocks(k)
        if k <= far:
            own_blocks(k)
        if far <= k <= far + 1:
            partner_blocks(k)
        if k == 1:
            from_x(2, 0)
            go_z(4, 0)
            go_sibling(2, 0)
            waiting["near"].append((2, 0))
        elif k <= far:
            for item, d in ring(k - 1):
                go_z(item, d)
        run(len(jobs) if k >= last - 1 else 1)
        for item, d in ring(k):
            from_z(item, d)
            if k >= far:
                go_z(item, d)
            go_sibling(item - 2, d)
            waiting["near"].append((item - 2, d))
        straight = k - 1 if k <= far + 1 else None
        if straight is not None:
            for d in offsets(straight):
                from_x(1, d)
                go_sibling(4, d)
                waiting["main"].append((3, d))
        for kind in (0, 1):
            if 0 <= k - 1 - kind <= far:
                for d in offsets(k - 1 - kind):
                    from_cross(kind, d)
                    go_sibling(5 + kind, d)
                    waiting["guest"].append((5 + kind, d))
        if k == 1:
            settle(kept.at[pl.ds(0, tok_n - 1)], bulk_s.at[0])
            settle(kept.at[pl.ds(0, tok_n - 1)], bulk_r.at[0])
            factor_copy.wait()
            lax.fori_loop(0, tok_n, sign_rows, 0)
            for load in loads[7:]:
                load.wait()
        run(len(jobs))
    for group in ("guest", "near", "main"):
        if waiting[group]:
            plan(group, list(waiting[group]))
    run(len(jobs))

    row_factor = jnp.concatenate(
        [
            factor[0, :, pl.ds(pl.multiple_of(col * block, block), 2 * block)],
            factor[0, :, 3 * block :],
            factor[1, :, pl.ds(pl.multiple_of(give * block, block), block)],
        ],
        axis=1,
    )

    def activate(m, carry):
        gate = acc[pl.ds(pl.multiple_of(m * 16, 16), 16), :]
        up = acc[pl.ds(pl.multiple_of(units + m * 16, 16), 16), :]
        silu = gate / (1.0 + jnp.exp(-gate))
        hidden[pl.ds(pl.multiple_of(m * 16, 16), 16), :] = (row_factor * silu * up).astype(BF16)
        return carry

    lax.fori_loop(0, units // 16, activate, 0)

    strips = units // 128

    def packed(rows):
        tail = rows[:, strips * 128 :]
        tail = jnp.concatenate([tail[: kept_n // 2], tail[kept_n // 2 :]], axis=1)
        return jnp.concatenate([rows[:, c * 128 : (c + 1) * 128] for c in range(strips)] + [tail], axis=0)

    def unpacked(strip):
        blocks = [strip[c * kept_n : (c + 1) * kept_n, :] for c in range(strips)]
        tail = strip[strips * kept_n :, :]
        return jnp.concatenate(blocks + [jnp.concatenate([tail[:, :64], tail[:, 64:]], axis=0)], axis=1)

    owners_step = max(tok_n // 2, 1)
    for b in range(tok_n // owners_step):
        rows = slice(b * owners_step * kept_n, (b + 1) * owners_step * kept_n)
        product = lax.dot_general(
            table[rows, :], hidden[...], (((1,), (1,)), ((), ())), preferred_element_type=F32
        )
        for i in range(owners_step):
            part[b * owners_step + i] = packed(product[i * kept_n : (i + 1) * kept_n, :]).astype(BF16)

    for peer in tok_peers:
        pltpu.make_async_remote_copy(
            src_ref=part.at[peer], dst_ref=got.at[tok], send_sem=bulk_s.at[1], recv_sem=bulk_r.at[1],
            device_id={"tok": peer}, device_id_type=MESH,
        ).start()
    got[tok] = part[tok]
    settle(got.at[pl.ds(0, tok_n - 1)], bulk_r.at[1])
    total = got[0].astype(F32)
    for j in range(1, tok_n):
        total = total + got[j].astype(F32)
    mine = (total * row_scale).astype(BF16)
    sk[tok] = mine

    for peer in tok_peers:
        pltpu.make_async_remote_copy(
            src_ref=sk.at[tok], dst_ref=sk.at[tok], send_sem=bulk_s.at[2], recv_sem=bulk_r.at[2],
            device_id={"tok": peer}, device_id_type=MESH,
        ).start()
    settle(sk.at[pl.ds(0, tok_n - 1)], bulk_r.at[2])
    every = jnp.concatenate([unpacked(sk[j]) for j in range(tok_n)], axis=0)
    gram = lax.dot_general(unpacked(mine), every, (((1,), (1,)), ((), ())), preferred_element_type=F32) * gram_scale

    tile_rows, tile_lanes = gs.shape[1:]
    across_n = gram.shape[1] // tile_lanes
    for t in range(hid_n):
        a, b = divmod(t, across_n)
        gs[t] = gram[a * tile_rows : (a + 1) * tile_rows, b * tile_lanes : (b + 1) * tile_lanes]

    def send_tile(peer):
        pltpu.make_async_remote_copy(
            src_ref=gs.at[peer], dst_ref=gr.at[hid], send_sem=bulk_s.at[3], recv_sem=bulk_r.at[3],
            device_id={"hid": peer}, device_id_type=MESH,
        ).start()

    to_hid_peers(send_tile)
    gr[hid] = gs[hid]
    settle(gr.at[pl.ds(0, hid_n - 1)], bulk_r.at[3])
    gf[hid] = jnp.sum(gr[...], axis=0)

    def send_sum(peer):
        pltpu.make_async_remote_copy(
            src_ref=gf.at[hid], dst_ref=gf.at[hid], send_sem=bulk_s.at[4], recv_sem=bulk_r.at[4],
            device_id={"hid": peer}, device_id_type=MESH,
        ).start()

    to_hid_peers(send_sum)
    for copy in sends:
        copy.wait_send()
    settle(part.at[pl.ds(0, tok_n - 1)], bulk_s.at[1])
    settle(sk.at[pl.ds(0, tok_n - 1)], bulk_s.at[2])
    settle(gs.at[pl.ds(0, hid_n - 1)], bulk_s.at[3])
    settle(gf.at[pl.ds(0, hid_n - 1)], bulk_r.at[4])
    for t in range(hid_n):
        a, b = divmod(t, across_n)
        out_ref[a * tile_rows : (a + 1) * tile_rows, b * tile_lanes : (b + 1) * tile_lanes] = gf[t]
    settle(gf.at[pl.ds(0, hid_n - 1)], bulk_s.at[4])


def per_device(tok_n, hid_n, activations, gate_weight, up_weight, row_signs, row_scales, kept_rows):
    tokens, width = activations.shape
    depth, units = gate_weight.shape
    kept_n = kept_rows.shape[0]
    zn = hid_n // 4
    far = zn // 2
    tile_lanes = kept_n * kept_n * tok_n // 8 // hid_n
    hbm = pl.BlockSpec(memory_space=pl.ANY)
    dma = pltpu.SemaphoreType.DMA
    return pl.pallas_call(
        functools.partial(fused, tok_n, hid_n, float(tokens * tok_n) ** -0.5, float(FF) ** -0.5),
        out_shape=jax.ShapeDtypeStruct((kept_n, kept_n * tok_n), F32),
        in_specs=[hbm] * 6,
        out_specs=pl.BlockSpec(memory_space=pltpu.VMEM),
        scratch_shapes=[
            pltpu.VMEM((hid_n // 2, 2, 4, tokens // 4, width), BF16),
            pltpu.VMEM((hid_n // 2, 2, tokens // 4, width), BF16),
            pltpu.VMEM((2 * units, depth), BF16),
            pltpu.VMEM((2 * units, tokens), F32),
            pltpu.VMEM((kept_n * tok_n, tokens), BF16),
            pltpu.VMEM((units, tokens), BF16),
            pltpu.VMEM((1, tokens), jnp.int32),
            pltpu.VMEM((1, tokens), F32),
            pltpu.VMEM((2, 1, tokens), F32),
            pltpu.VMEM((tok_n, 1, kept_n), jnp.int32),
            pltpu.VMEM((tok_n, kept_n * units // 128, 128), BF16),
            pltpu.VMEM((tok_n, kept_n * units // 128, 128), BF16),
            pltpu.VMEM((tok_n, kept_n * units // 128, 128), BF16),
            pltpu.VMEM((hid_n, 8, tile_lanes), F32),
            pltpu.VMEM((hid_n, 8, tile_lanes), F32),
            pltpu.VMEM((hid_n, 8, tile_lanes), F32),
            dma((9,)),
            dma((2, far, 5)),
            dma((2, far, 5)),
            dma((3, 2 * far)),
            dma((3, 2 * far)),
            dma((2, 2 * far)),
            dma((2, 2 * far)),
            dma((7, 2 * far)),
            dma((7, 2 * far)),
            dma((6,)),
            dma((6,)),
        ],
        compiler_params=pltpu.CompilerParams(
            collective_id=0, has_side_effects=True, vmem_limit_bytes=60 * 1024 * 1024
        ),
        name="sketch_gram",
    )(
        activations, gate_weight.T, up_weight.T,
        row_signs.reshape(1, -1), row_scales.reshape(1, -1), kept_rows.reshape(1, -1),
    )


def solution(mesh):
    placed = (P("tok", "hid"), P(None, "hid"), P(None, "hid"), P("tok"), P("tok"), P("tok"))
    return jax.shard_map(
        functools.partial(per_device, mesh.shape["tok"], mesh.shape["hid"]),
        mesh=mesh, in_specs=placed, out_specs=P("tok", None), check_vma=False,
    )
```
